512 devices in a mesh: azimuth: 64 (over x, z), span: 8 (over y, core).
Axes of the slice: x: 4, y: 4, z: 16, core: 2. Of those that a mesh axis runs over, the one named last changes fastest.
Arguments:
- sensitivity: float32 [3, 256, 128, 512], P(None, 'azimuth', 'span'), may hold values from -6 to 6
- stiffness: float32 [256, 128, 512], P('azimuth', 'span'), may hold values from 0.05 to 2
- spring: float32 [256, 128, 512], P('azimuth', 'span'), may hold values from 0.05 to 0.5
- shear: float32 [3, 256, 128, 512], P(None, 'azimuth', 'span'), may hold values from -0.3 to 0.3
- interface: int32 [256, 128, 4], P('azimuth', 'span'), may hold values 0 or 1
- live_blocks: int32 [64, 8], P('azimuth', 'span'), may hold values from 1 to 4, as said below
Outputs:
- solution_field: float32 [3, 256, 128, 512], P(None, 'azimuth', 'span')
- residual: float32 [3, 256, 128, 512], P(None, 'azimuth', 'span')
The draws below stay inside these ranges and needn't reach their ends.
Inputs may be any that keep to these rules, and one draw needn't show every extreme that they name: `live_blocks`: each device's number of live node blocks; one device holds all 4 in every draw.
All inputs are finite; a program needn't handle non-finite values. No bound on the sum of `interface` on one device may be relied on, other than what follows from the above.
Results may differ from the reference program's by a relative error of at most 0.0003.
Values sent between devices are 32-bit elements; how exact they have to be, the bound alone decides.
No kernel may reach another device: no remote copies, remote signals or barrier semaphores. Data moves between devices by JAX's collectives and lax.ppermute only.
A program may use at most 64 MiB of HBM per device.

```python
import math
import jax
import jax.numpy as jnp
from jax import lax

CA = 4
CS = 16
BLOCK = 128
NB = 4
ITERS = 3
NA = 256
NS = 128
NZ = 512
RANKS_AZ = 64
RANKS_SPAN = 8


def draw_live_blocks(key, part):
    counts = jax.random.randint(key, (RANKS_AZ, RANKS_SPAN), max(1, NB // 4), NB + 1)
    return counts.at[0, 0].set(NB).astype(jnp.int32)


def touch_ends(values, rng, least, top_value):
    shape = values.shape
    spot = [jax.random.randint(jax.random.fold_in(rng, axis), (), 0, shape[axis]) for axis in range(len(shape))]
    values = values.at[tuple(spot)].set(least)
    longest = shape.index(max(shape))
    spot[longest] = (spot[longest] + 1) % shape[longest]
    return values.at[tuple(spot)].set(top_value)


def block_levels(key, extent, pieces, low, top_value):
    level, own = 1.0, jax.random.fold_in(key, 6)
    for dim, blocks in pieces:
        heights = jnp.exp(jax.random.uniform(jax.random.fold_in(own, dim), (blocks,), jnp.float32, low / len(pieces), top_value / len(pieces)))
        level = level * jnp.repeat(heights, extent[dim] // blocks).reshape([-1 if axis == dim else 1 for axis in range(len(extent))])
    return level


def scatter_about(own_key, shape, spread, reach, cuts=(), kind=jnp.bfloat16):
    entries = jax.random.normal(own_key, shape, jnp.float32) * spread
    if len(cuts) > 0:
        entries = block_levels(own_key, shape, cuts, -0.22, 0.18) * entries
    return jnp.clip(entries, min=-reach, max=reach).astype(kind)


def setup_inputs(seed: int = 0) -> dict:
    streams_of = jax.random.split(jax.random.key(seed), 7)
    return {
        "sensitivity": scatter_about(streams_of[0], (3, NA, NS, NZ), 1.0, 6.0, ((1, 64), (2, 8)), jnp.float32),
        "stiffness": jnp.clip(jnp.exp(math.log(2.0) - 3.6888794 * jax.random.uniform(streams_of[1], (NA, NS, NZ), jnp.float32) ** block_levels(streams_of[1], (NA, NS, NZ), ((0, 64), (1, 8)), -0.2, 0.2)), 0.05, 2.0),
        "spring": jnp.clip(jnp.exp(math.log(0.5) - 2.3025851 * jax.random.uniform(streams_of[2], (NA, NS, NZ), jnp.float32) ** block_levels(streams_of[2], (NA, NS, NZ), ((0, 64), (1, 8)), -0.2, 0.2)), 0.05, 0.5),
        "shear": jnp.clip(jax.random.uniform(streams_of[3], (3, NA, NS, NZ), jnp.float32, -0.3, 0.3) * block_levels(streams_of[3], (3, NA, NS, NZ), ((1, 64), (2, 8)), -0.4, 0.0), -0.3, 0.3),
        "interface": touch_ends((jax.random.randint(streams_of[4], (NA, NS, NB), 0, 4) < 1).astype(jnp.int32), jax.random.fold_in(streams_of[4], 1), 0, 1),
        "live_blocks": draw_live_blocks(jax.random.fold_in(streams_of[6], 71), 0),
    }


penalty_weight = 4.0


def ahead(field, axis):
    count = field.shape[axis]
    rest = lax.slice_in_dim(field, 1, count, axis=axis)
    return jnp.concatenate([rest, jnp.zeros_like(lax.slice_in_dim(field, 0, 1, axis=axis))], axis)


def behind(field, axis):
    count = field.shape[axis]
    rest = lax.slice_in_dim(field, 0, count - 1, axis=axis)
    return jnp.concatenate([jnp.zeros_like(lax.slice_in_dim(field, 0, 1, axis=axis)), rest], axis)


def reference(sensitivity, stiffness, spring, shear, interface, live_blocks):
    counts = jnp.repeat(jnp.repeat(live_blocks, CA, axis=0), CS, axis=1)
    zpos = lax.broadcasted_iota(jnp.int32, stiffness.shape, 2)
    live = (zpos < counts[:, :, None] * BLOCK).astype(jnp.float32)
    inter = jnp.repeat(interface, BLOCK, axis=2).astype(jnp.float32)
    k = stiffness
    w_ap = live * jnp.roll(live, -1, 0) * (k + jnp.roll(k, -1, 0)) * 0.5
    w_am = live * jnp.roll(live, 1, 0) * (k + jnp.roll(k, 1, 0)) * 0.5
    w_sp = live * ahead(live, 1) * (k + ahead(k, 1)) * 0.5
    w_sm = live * behind(live, 1) * (k + behind(k, 1)) * 0.5
    w_zp = live * ahead(live, 2) * (k + ahead(k, 2)) * 0.5
    w_zm = live * behind(live, 2) * (k + behind(k, 2)) * 0.5

    def operate(field):
        lap = w_ap * (field - jnp.roll(field, -1, 1)) + w_am * (field - jnp.roll(field, 1, 1))
        lap = lap + w_sp * (field - ahead(field, 2)) + w_sm * (field - behind(field, 2))
        lap = lap + w_zp * (field - ahead(field, 3)) + w_zm * (field - behind(field, 3))
        coupled = jnp.stack([field[0] + shear[0] * field[1] + shear[1] * field[2],
                             shear[0] * field[0] + field[1] + shear[2] * field[2],
                             shear[1] * field[0] + shear[2] * field[1] + field[2]]) * spring
        return live * (lap + coupled + penalty_weight * inter * field)

    residual = live * sensitivity
    solution_field = jnp.zeros_like(residual)
    direction = residual
    norm_now = jnp.sum(residual * residual)
    for step in range(ITERS):
        image = operate(direction)
        alpha = norm_now / jnp.sum(direction * image)
        solution_field = solution_field + alpha * direction
        residual = residual - alpha * image
        norm_next = jnp.sum(residual * residual)
        direction = residual + (norm_next / norm_now) * direction
        norm_now = norm_next
    return solution_field, residual
```

```python
import functools

import jax
import jax.numpy as jnp
from jax import lax
from jax.experimental import pallas as pl
from jax.experimental.pallas import tpu as pltpu
from jax.sharding import PartitionSpec as P


ITERS = 3
penalty_weight = 4.0
SHIFT = 5.0
SAFE = 0.01
F32 = jnp.float32
VMEM = pl.BlockSpec(memory_space=pltpu.VMEM)
SMEM = pl.BlockSpec(memory_space=pltpu.SMEM)


def padded_2(x, sides, width):
    for axis, dim in sides:
        peers, length = (lax.axis_size(axis), x.shape[dim])
        up = [(i, (i + 1) % peers) for i in range(peers)]
        down = [(j, i) for i, j in up]
        last = lax.slice_in_dim(x, length - width, length, axis=dim)
        leading = lax.slice_in_dim(x, 0, width, axis=dim)
        before = lax.ppermute(last, axis, up)
        after = lax.ppermute(leading, axis, down)
        x = jnp.concatenate([before, x, after], axis=dim)
    return x


def ahead(field, axis):
    count = field.shape[axis]
    rest = lax.slice_in_dim(field, 1, count, axis=axis)
    return jnp.concatenate([rest, jnp.zeros_like(lax.slice_in_dim(field, 0, 1, axis=axis))], axis)


def behind(field, axis):
    count = field.shape[axis]
    rest = lax.slice_in_dim(field, 0, count - 1, axis=axis)
    return jnp.concatenate([jnp.zeros_like(lax.slice_in_dim(field, 0, 1, axis=axis)), rest], axis)


def coupling(field, shear, spring):
    return (
        jnp.stack(
            [
                field[0] + shear[0] * field[1] + shear[1] * field[2],
                shear[0] * field[0] + field[1] + shear[2] * field[2],
                shear[1] * field[0] + shear[2] * field[1] + field[2],
            ]
        )
        * spring
    )


def stepwise(sensitivity, stiffness, spring, shear, live, inter):
    rows_az, rows_span, slots = stiffness.shape
    padded = padded_2(jnp.stack([stiffness, live]), (("azimuth", 1), ("span", 2)), 1)
    kpad = padded[0]
    lpad = padded[1]
    w_ap = live * lpad[2:, 1:-1] * (stiffness + kpad[2:, 1:-1]) * 0.5
    w_am = live * lpad[:-2, 1:-1] * (stiffness + kpad[:-2, 1:-1]) * 0.5
    w_sp = live * lpad[1:-1, 2:] * (stiffness + kpad[1:-1, 2:]) * 0.5
    w_sm = live * lpad[1:-1, :-2] * (stiffness + kpad[1:-1, :-2]) * 0.5
    span_rank = lax.axis_index("span")
    span_count = lax.axis_size("span")
    row = lax.broadcasted_iota(jnp.int32, stiffness.shape, 1)
    top_edge = jnp.logical_and(span_rank == span_count - 1, row == rows_span - 1)
    low_edge = jnp.logical_and(span_rank == 0, row == 0)
    w_sp = jnp.where(top_edge, 0.0, w_sp)
    w_sm = jnp.where(low_edge, 0.0, w_sm)
    w_zp = live * ahead(live, 2) * (stiffness + ahead(stiffness, 2)) * 0.5
    w_zm = live * behind(live, 2) * (stiffness + behind(stiffness, 2)) * 0.5
    residual = live * sensitivity
    solution_field = jnp.zeros_like(residual)

    def squares(vector):
        return lax.psum(jnp.sum(vector * vector), ("azimuth", "span"))

    def iteration(step, carry):
        solution_field, residual, direction, norm_now = carry
        extended = padded_2(direction, (("azimuth", 1), ("span", 2)), 1)
        next_az = extended[:, 2:, 1:-1]
        prev_az = extended[:, :-2, 1:-1]
        next_span = extended[:, 1:-1, 2:]
        prev_span = extended[:, 1:-1, :-2]
        lap = w_ap * (direction - next_az) + w_am * (direction - prev_az)
        lap = lap + w_sp * (direction - next_span) + w_sm * (direction - prev_span)
        lap = (
            lap
            + w_zp * (direction - ahead(direction, 3))
            + w_zm * (direction - behind(direction, 3))
        )
        coupled = coupling(direction, shear, spring)
        image = live * (lap + coupled + penalty_weight * inter * direction)
        alpha = norm_now / lax.psum(jnp.sum(direction * image), ("azimuth", "span"))
        solution_field = solution_field + alpha * direction
        residual = residual - alpha * image
        norm_next = squares(residual)
        direction = residual + norm_next / norm_now * direction
        return solution_field, residual, direction, norm_next

    carry = (solution_field, residual, residual, squares(residual))
    carry = lax.fori_loop(0, ITERS, iteration, carry)
    return carry[0], carry[1]


def call(kernel, shapes, n_in, smem=()):
    return pl.pallas_call(
        kernel,
        out_shape=[jax.ShapeDtypeStruct(s, F32) for s in shapes],
        in_specs=[SMEM if i in smem else VMEM for i in range(n_in)],
        out_specs=[VMEM] * len(shapes),
        compiler_params=pltpu.CompilerParams(vmem_limit_bytes=24 << 20),
    )


def pack_kernel(blocks_ref, s_ref, k_ref, r_ref, kl_ref, lo_ref, hi_ref, sl_ref, sh_ref):
    n_az, n_sp, slots = k_ref.shape
    zpos = lax.broadcasted_iota(jnp.int32, (n_sp, slots), 1)
    live = zpos < blocks_ref[0, 0] * 128
    for a in range(n_az):
        for c in range(4):
            src = s_ref[c, a] if c < 3 else k_ref[a]
            v = jnp.where(live, src, 0.0)
            if c < 3:
                r_ref[c, a] = v
            else:
                kl_ref[a] = v
            if a == 0:
                lo_ref[c] = v
            if a == n_az - 1:
                hi_ref[c] = v
            row = c * n_az + a
            sl_ref[row : row + 1, :] = v[0:1, :]
            sh_ref[row : row + 1, :] = v[n_sp - 1 : n_sp, :]


def span_next(x, edge):
    n = x.shape[0]
    row = lax.broadcasted_iota(jnp.int32, x.shape, 0)
    return jnp.where(row == n - 1, edge, pltpu.roll(x, n - 1, 0))


def span_prev(x, edge):
    row = lax.broadcasted_iota(jnp.int32, x.shape, 0)
    return jnp.where(row == 0, edge, pltpu.roll(x, 1, 0))


def shifted(u_ref, ap_ref, an_ref, sp_ref, sn_ref, w, a, c):
    n_az = u_ref.shape[1]
    slots = u_ref.shape[3]
    u = u_ref[c, a]
    row = c * n_az + a
    nxt = u_ref[c, a + 1] if a + 1 < n_az else an_ref[c]
    prv = u_ref[c, a - 1] if a > 0 else ap_ref[c]
    acc = w[0] * nxt + w[1] * prv
    acc = acc + w[2] * span_next(u, sn_ref[row : row + 1, :])
    acc = acc + w[3] * span_prev(u, sp_ref[row : row + 1, :])
    acc = acc + w[4] * pltpu.roll(u, slots - 1, 1) + w[5] * pltpu.roll(u, 1, 1)
    return u, acc


def image_of(u_ref, halos, w, diag, off, a):
    ap_ref, an_ref, sp_ref, sn_ref = halos
    parts = [shifted(u_ref, ap_ref, an_ref, sp_ref, sn_ref, w, a, c) for c in range(3)]
    u = [p[0] for p in parts]
    mixed = [off[0] * u[1] + off[1] * u[2], off[0] * u[0] + off[2] * u[2], off[1] * u[0] + off[2] * u[1]]
    return u, [diag * u[c] + mixed[c] - parts[c][1] for c in range(3)]


def emit_edges(image, a, n_az, lo_ref, hi_ref, sl_ref, sh_ref):
    for c in range(3):
        v = image[c]
        n_sp = v.shape[0]
        if a == 0:
            lo_ref[c] = v
        if a == n_az - 1:
            hi_ref[c] = v
        row = c * n_az + a
        sl_ref[row : row + 1, :] = v[0:1, :]
        sh_ref[row : row + 1, :] = v[n_sp - 1 : n_sp, :]


def first_kernel(r_ref, kl_ref, spring_ref, shear_ref, inter_ref, ap, an, sp, sn, u_ref, w_ref, lo, hi, sl, sh):
    n_az, n_sp, slots = kl_ref.shape
    lane = lax.broadcasted_iota(jnp.int32, (n_sp, slots), 1)
    width = slots // inter_ref.shape[2]
    for a in range(n_az):
        k = kl_ref[a]
        live = k > 0.0
        row = 3 * n_az + a
        near = [
            kl_ref[a + 1] if a + 1 < n_az else an[3],
            kl_ref[a - 1] if a > 0 else ap[3],
            span_next(k, sn[row : row + 1, :]),
            span_prev(k, sp[row : row + 1, :]),
            jnp.where(lane == slots - 1, 0.0, pltpu.roll(k, slots - 1, 1)),
            jnp.where(lane == 0, 0.0, pltpu.roll(k, 1, 1)),
        ]
        w = [jnp.where(jnp.logical_and(live, n > 0.0), (k + n) * 0.5, 0.0) for n in near]
        spring = jnp.where(live, spring_ref[a], 0.0)
        inter = jnp.concatenate(
            [jnp.broadcast_to(inter_ref[a][:, b : b + 1], (n_sp, width)) for b in range(slots // width)], axis=1
        )
        extra = jnp.where(live, penalty_weight * inter - SHIFT, 0.0)
        diag = (w[0] + w[1]) + (w[2] + w[3]) + (w[4] + w[5]) + (spring + extra)
        off = [shear_ref[i, a] * spring for i in range(3)]
        for i, v in enumerate(w + [diag] + off):
            w_ref[i, a] = v
        _, image = image_of(r_ref, (ap, an, sp, sn), w, diag, off, a)
        for c in range(3):
            u_ref[c, a] = image[c]
        emit_edges(image, a, n_az, lo, hi, sl, sh)


def next_kernel(u_ref, w_ref, ap, an, sp, sn, v_ref, lo, hi, sl, sh):
    n_az = u_ref.shape[1]
    for a in range(n_az):
        w = [w_ref[i, a] for i in range(10)]
        _, image = image_of(u_ref, (ap, an, sp, sn), w[:6], w[6], w[7:], a)
        for c in range(3):
            v_ref[c, a] = image[c]
        emit_edges(image, a, n_az, lo, hi, sl, sh)


PAIRS = ((0, 0), (0, 1), (0, 2), (0, 3), (1, 1), (1, 2), (1, 3), (2, 2), (2, 3), (3, 3))


def folded(x):
    n, m = x.shape
    x = x.reshape(n // 8, 8, m).sum(0) if n > 8 else x
    out = x[:, 0:128]
    for b in range(1, m // 128):
        out = out + x[:, b * 128 : (b + 1) * 128]
    return out


def last_kernel(u0_ref, u1_ref, u2_ref, w_ref, ap, an, sp, sn, u3_ref, sums_ref):
    n_az = u2_ref.shape[1]
    acc = [jnp.zeros((8, 128), F32) for _ in PAIRS]
    for a in range(n_az):
        w = [w_ref[i, a] for i in range(10)]
        u2, u3 = image_of(u2_ref, (ap, an, sp, sn), w[:6], w[6], w[7:], a)
        for c in range(3):
            u3_ref[c, a] = u3[c]
            v = [u0_ref[c, a], u1_ref[c, a], u2[c], u3[c]]
            for n, (i, j) in enumerate(PAIRS):
                acc[n] = acc[n] + folded(v[i] * v[j])
    lane = lax.broadcasted_iota(jnp.int32, (8, 128), 1)
    total = jnp.zeros((8, 128), F32)
    for n in range(len(PAIRS)):
        s = jnp.sum(jnp.sum(acc[n], axis=0, keepdims=True), axis=1, keepdims=True)
        total = jnp.where(lane == n, s, total)
    sums_ref[...] = total


def coefficients(rows):
    lane = lax.broadcasted_iota(jnp.int32, (8, 128), 1)
    row = jnp.broadcast_to(jnp.sum(rows, axis=0, keepdims=True), (8, 128))

    def entry(n):
        return jnp.broadcast_to(jnp.sum(jnp.where(lane == n, row, 0.0), axis=1, keepdims=True), (8, 128))

    g = {p: entry(n) for n, p in enumerate(PAIRS)}
    n0 = g[0, 0]
    m10, m20, m30 = g[0, 1] / n0, g[0, 2] / n0, g[0, 3] / n0
    n1 = g[1, 1] - m10 * g[0, 1]
    t21 = g[1, 2] - m10 * g[0, 2]
    t31 = g[1, 3] - m10 * g[0, 3]
    m21, m31 = t21 / n1, t31 / n1
    n2 = g[2, 2] - m20 * g[0, 2] - m21 * t21
    t32 = g[2, 3] - m20 * g[0, 3] - m21 * t31
    m32 = t32 / n2
    n3 = g[3, 3] - m30 * g[0, 3] - m31 * t31 - m32 * t32
    b0, b1, b2 = SHIFT + m10, SHIFT + m21 - m10, SHIFT + m32 - m21
    g1, g2 = n1 / n0, n2 / n1
    a0 = 1.0 / b0
    a1 = 1.0 / (b1 - g1 * a0)
    a2 = 1.0 / (b2 - g2 * a1)
    safe = jnp.logical_and(
        jnp.logical_and(n1 > SAFE * g[1, 1], n2 > SAFE * g[2, 2]),
        jnp.logical_and(n3 > SAFE * g[3, 3], jnp.logical_and(a1 > 0.0, a2 > 0.0)),
    )
    f = {"m10": m10, "m20": m20, "m21": m21, "m30": m30, "m31": m31, "m32": m32}
    f["e1"], f["e2"] = a0 * g1, a1 * g2
    f["x0"], f["x1"], f["x2"] = a0, -(a0 * a1), a0 * a1 * a2
    f["r3"] = -(a0 * a1 * a2)
    return f, safe


def final_kernel(rows_ref, u0_ref, u1_ref, u2_ref, u3_ref, x_ref, r_ref, safe_ref):
    f, safe = coefficients(rows_ref[...])
    safe_ref[...] = jnp.where(safe, 1.0, 0.0)
    n_az, n_sp, slots = u0_ref.shape[1:]
    f = {key: jnp.concatenate([jnp.concatenate([v] * (n_sp // 8), 0)] * (slots // 128), 1) for key, v in f.items()}
    for c in range(3):
        for a in range(n_az):
            u0, u1, u2, u3 = u0_ref[c, a], u1_ref[c, a], u2_ref[c, a], u3_ref[c, a]
            q1 = u1 - f["m10"] * u0
            q2 = u2 - f["m21"] * q1 - f["m20"] * u0
            q3 = u3 - f["m32"] * q2 - f["m31"] * q1 - f["m30"] * u0
            p1 = q1 - f["e1"] * u0
            p2 = q2 - f["e2"] * p1
            x_ref[c, a] = f["x0"] * u0 + f["x1"] * p1 + f["x2"] * p2
            r_ref[c, a] = f["r3"] * q3


def exchange(lo, hi, sl, sh):
    n_az, n_sp = lax.axis_size("azimuth"), lax.axis_size("span")
    up = [(i, (i + 1) % n_az) for i in range(n_az)]
    prv = lax.ppermute(hi, "azimuth", up)
    nxt = lax.ppermute(lo, "azimuth", [(j, i) for i, j in up])
    rise = [(i, i + 1) for i in range(n_sp - 1)]
    sp = lax.ppermute(sh, "span", rise)
    sn = lax.ppermute(sl, "span", [(j, i) for i, j in rise])
    return prv, nxt, sp, sn


def everywhere(row, axis):
    n = lax.axis_size(axis)
    return lax.all_to_all(jnp.broadcast_to(row, (n, 128)), axis, 0, 0, tiled=True)


def on_device(sensitivity, stiffness, spring, shear, interface, live_blocks):
    rows_az, rows_span, slots = stiffness.shape
    blocks = interface.shape[2]
    width = slots // blocks
    field = (3, rows_az, rows_span, slots)
    layer = (3, rows_span, slots)
    strip = (3 * rows_az, slots)
    r, kl, lo, hi, sl, sh = call(
        pack_kernel,
        [field, field[1:], (4,) + layer[1:], (4,) + layer[1:], (4 * rows_az, slots), (4 * rows_az, slots)],
        3,
        smem=(0,),
    )(live_blocks, sensitivity, stiffness)
    u1, w, lo, hi, sl, sh = call(first_kernel, [field, (10,) + field[1:], layer, layer, strip, strip], 9)(
        r, kl, spring, shear, interface.astype(F32), *exchange(lo, hi, sl, sh)
    )
    u2, lo, hi, sl, sh = call(next_kernel, [field, layer, layer, strip, strip], 6)(u1, w, *exchange(lo, hi, sl, sh))
    u3, sums = call(last_kernel, [field, (8, 128)], 8)(r, u1, u2, w, *exchange(lo, hi, sl, sh))
    sums = jnp.sum(everywhere(sums[0:1], "span"), axis=0, keepdims=True)
    rows = everywhere(sums, "azimuth")
    x, res, safe = call(final_kernel, [field, field, (8, 128)], 5)(rows, r, u1, u2, u3)

    def guarded():
        zpos = lax.broadcasted_iota(jnp.int32, stiffness.shape, 2)
        live = (zpos < live_blocks[0, 0] * width).astype(F32)
        inter = jnp.broadcast_to(interface[:, :, :, None], (rows_az, rows_span, blocks, width))
        inter = inter.reshape(stiffness.shape).astype(F32)
        return stepwise(sensitivity, stiffness, spring, shear, live, inter)

    return lax.cond(safe[0, 0] > 0.5, lambda: (x, res), guarded)


def solution(mesh):
    return jax.shard_map(
        on_device,
        mesh=mesh,
        in_specs=(
            P(None, "azimuth", "span", None),
            P("azimuth", "span", None),
            P("azimuth", "span", None),
            P(None, "azimuth", "span", None),
            P("azimuth", "span", None),
            P("azimuth", "span"),
        ),
        out_specs=(P(None, "azimuth", "span", None), P(None, "azimuth", "span", None)),
        check_vma=False,
    )
```

```python
import functools

import jax
import jax.numpy as jnp
from jax import lax
from jax.experimental import pallas as pl
from jax.experimental.pallas import tpu as pltpu
from jax.sharding import PartitionSpec as P


ITERS = 3
penalty_weight = 4.0
SHIFT = 5.0
SAFE = 0.01
F32 = jnp.float32
VMEM = pl.BlockSpec(memory_space=pltpu.VMEM)
SMEM = pl.BlockSpec(memory_space=pltpu.SMEM)


def padded_2(x, sides, width):
    for axis, dim in sides:
        peers, length = (lax.axis_size(axis), x.shape[dim])
        up = [(i, (i + 1) % peers) for i in range(peers)]
        down = [(j, i) for i, j in up]
        last = lax.slice_in_dim(x, length - width, length, axis=dim)
        leading = lax.slice_in_dim(x, 0, width, axis=dim)
        before = lax.ppermute(last, axis, up)
        after = lax.ppermute(leading, axis, down)
        x = jnp.concatenate([before, x, after], axis=dim)
    return x


def ahead(field, axis):
    count = field.shape[axis]
    rest = lax.slice_in_dim(field, 1, count, axis=axis)
    return jnp.concatenate([rest, jnp.zeros_like(lax.slice_in_dim(field, 0, 1, axis=axis))], axis)


def behind(field, axis):
    count = field.shape[axis]
    rest = lax.slice_in_dim(field, 0, count - 1, axis=axis)
    return jnp.concatenate([jnp.zeros_like(lax.slice_in_dim(field, 0, 1, axis=axis)), rest], axis)


def coupling(field, shear, spring):
    return (
        jnp.stack(
            [
                field[0] + shear[0] * field[1] + shear[1] * field[2],
                shear[0] * field[0] + field[1] + shear[2] * field[2],
                shear[1] * field[0] + shear[2] * field[1] + field[2],
            ]
        )
        * spring
    )


def stepwise(sensitivity, stiffness, spring, shear, live, inter):
    rows_az, rows_span, slots = stiffness.shape
    padded = padded_2(jnp.stack([stiffness, live]), (("azimuth", 1), ("span", 2)), 1)
    kpad = padded[0]
    lpad = padded[1]
    w_ap = live * lpad[2:, 1:-1] * (stiffness + kpad[2:, 1:-1]) * 0.5
    w_am = live * lpad[:-2, 1:-1] * (stiffness + kpad[:-2, 1:-1]) * 0.5
    w_sp = live * lpad[1:-1, 2:] * (stiffness + kpad[1:-1, 2:]) * 0.5
    w_sm = live * lpad[1:-1, :-2] * (stiffness + kpad[1:-1, :-2]) * 0.5
    span_rank = lax.axis_index("span")
    span_count = lax.axis_size("span")
    row = lax.broadcasted_iota(jnp.int32, stiffness.shape, 1)
    top_edge = jnp.logical_and(span_rank == span_count - 1, row == rows_span - 1)
    low_edge = jnp.logical_and(span_rank == 0, row == 0)
    w_sp = jnp.where(top_edge, 0.0, w_sp)
    w_sm = jnp.where(low_edge, 0.0, w_sm)
    w_zp = live * ahead(live, 2) * (stiffness + ahead(stiffness, 2)) * 0.5
    w_zm = live * behind(live, 2) * (stiffness + behind(stiffness, 2)) * 0.5
    residual = live * sensitivity
    solution_field = jnp.zeros_like(residual)

    def squares(vector):
        return lax.psum(jnp.sum(vector * vector), ("azimuth", "span"))

    def iteration(step, carry):
        solution_field, residual, direction, norm_now = carry
        extended = padded_2(direction, (("azimuth", 1), ("span", 2)), 1)
        next_az = extended[:, 2:, 1:-1]
        prev_az = extended[:, :-2, 1:-1]
        next_span = extended[:, 1:-1, 2:]
        prev_span = extended[:, 1:-1, :-2]
        lap = w_ap * (direction - next_az) + w_am * (direction - prev_az)
        lap = lap + w_sp * (direction - next_span) + w_sm * (direction - prev_span)
        lap = (
            lap
            + w_zp * (direction - ahead(direction, 3))
            + w_zm * (direction - behind(direction, 3))
        )
        coupled = coupling(direction, shear, spring)
        image = live * (lap + coupled + penalty_weight * inter * direction)
        alpha = norm_now / lax.psum(jnp.sum(direction * image), ("azimuth", "span"))
        solution_field = solution_field + alpha * direction
        residual = residual - alpha * image
        norm_next = squares(residual)
        direction = residual + norm_next / norm_now * direction
        return solution_field, residual, direction, norm_next

    carry = (solution_field, residual, residual, squares(residual))
    carry = lax.fori_loop(0, ITERS, iteration, carry)
    return carry[0], carry[1]


DEPTH = 3
FIELDS = 8
TILE = 8


def call(kernel, shapes, n_in, smem=(), scratch=()):
    return pl.pallas_call(
        kernel,
        out_shape=[jax.ShapeDtypeStruct(s, F32) for s in shapes],
        in_specs=[SMEM if i in smem else VMEM for i in range(n_in)],
        out_specs=[VMEM] * len(shapes),
        scratch_shapes=[pltpu.VMEM(s, F32) for s in scratch],
        compiler_params=pltpu.CompilerParams(vmem_limit_bytes=32 << 20),
    )


def reach(f):
    return DEPTH if f < 4 else DEPTH - 1


def place(f, d):
    return f * DEPTH + d - 1 if f < 4 else 4 * DEPTH + (f - 4) * (DEPTH - 1) + d - 1


def pack_kernel(blocks_ref, s_ref, k_ref, spring_ref, shear_ref, inter_ref, own_ref, lo_ref, hi_ref, sl_ref, sh_ref):
    n_az, n_sp, slots = k_ref.shape
    blocks = inter_ref.shape[2]
    width = slots // blocks
    zpos = lax.broadcasted_iota(jnp.int32, (n_sp, slots), 1)
    live = zpos < blocks_ref[0, 0] * width
    for a in range(n_az):
        spring = spring_ref[a]
        inter = inter_ref[a].astype(F32)
        inter = jnp.concatenate([jnp.broadcast_to(inter[:, b : b + 1], (n_sp, width)) for b in range(blocks)], axis=1)
        fields = [s_ref[c, a] for c in range(3)] + [k_ref[a], spring + penalty_weight * inter]
        fields += [shear_ref[i, a] * spring for i in range(3)]
        for f, v in enumerate(fields):
            v = jnp.where(live, v, 0.0)
            own_ref[f, a] = v
            if a + 1 <= reach(f):
                lo_ref[place(f, a + 1)] = v
            if n_az - a <= reach(f):
                hi_ref[place(f, n_az - a)] = v
            sl_ref[f * n_az + a] = v[:TILE]
            sh_ref[f * n_az + a] = v[n_sp - TILE :]


def sublane(slots):
    return lax.broadcasted_iota(jnp.int32, (TILE, slots), 0)


def turn(x, shift, axis):
    shift = shift % x.shape[axis]
    return pltpu.roll(x, shift, axis) if shift else x


def beside(sn_ref, sp_ref, n):
    after, before = sn_ref[n], sp_ref[n]
    return jnp.where(sublane(after.shape[1]) < TILE // 2, after, before)


def corner_kernel(sp_ref, sn_ref, cl_ref, ch_ref):
    n_az = sp_ref.shape[0] // FIELDS
    s = sublane(sp_ref.shape[2])
    for out, one, two in ((cl_ref, 0, 1), (ch_ref, n_az - 1, n_az - 2)):
        for f in range(4):
            near = beside(sn_ref, sp_ref, f * n_az + one)
            far = beside(sn_ref, sp_ref, f * n_az + two)
            out[f] = jnp.where(s == 2, turn(far, 2, 0), jnp.where(s == 5, turn(far, -2, 0), near))
        packed = jnp.zeros(near.shape, F32)
        for j in range(4):
            near = beside(sn_ref, sp_ref, (4 + j) * n_az + one)
            packed = jnp.where(s == j, turn(near, j, 0), jnp.where(s == TILE - 1 - j, turn(near, -j, 0), packed))
        out[4] = packed


PAIRS = ((0, 0), (0, 1), (0, 2), (0, 3), (1, 1), (1, 2), (1, 3), (2, 2), (2, 3), (3, 3))


def folded(x):
    n, m = x.shape
    x = x.reshape(n // 8, 8, m).sum(0) if n > 8 else x
    out = x[:, 0:128]
    for b in range(1, m // 128):
        out = out + x[:, b * 128 : (b + 1) * 128]
    return out


def basis_kernel(own, ap, an, sp, sn, cp, cn, u1_ref, u2_ref, u3_ref, sums_ref, wa_ref, ws_ref, wz_ref, diag_ref):
    n_az, n_sp, slots = own.shape[1:]
    s = sublane(slots)
    lane = lax.broadcasted_iota(jnp.int32, (n_sp + TILE, slots), 1)

    def field(f, a):
        if 0 <= a < n_az:
            return jnp.concatenate([own[f, a], beside(sn, sp, f * n_az + a)], axis=0)
        side, corner, d = (an, cn, a - n_az + 1) if a >= n_az else (ap, cp, -a)
        if f < 4:
            tile = corner[f]
            if d == 2:
                tile = jnp.where(s < TILE // 2, turn(tile, -2, 0), turn(tile, 2, 0))
        else:
            j = f - 4
            tile = corner[4]
            tile = jnp.where(s < TILE // 2, turn(tile, -j, 0), turn(tile, j, 0))
        return jnp.concatenate([side[place(f, d)], tile], axis=0)

    def face(k, near):
        return jnp.where(jnp.minimum(k, near) > 0.0, (k + near) * 0.5, 0.0)

    for a in range(-DEPTH, n_az + DEPTH - 1):
        wa_ref[a + DEPTH] = face(field(3, a), field(3, a + 1))
    for a in range(1 - DEPTH, n_az + DEPTH - 1):
        k = field(3, a)
        ws = face(k, turn(k, -1, 0))
        wz = face(k, jnp.where(lane == slots - 1, 0.0, turn(k, -1, 1)))
        n = a + DEPTH - 1
        ws_ref[n], wz_ref[n] = ws, wz
        total = (wa_ref[n] + wa_ref[n + 1]) + (ws + turn(ws, 1, 0)) + (wz + turn(wz, 1, 1))
        diag_ref[n] = total + (field(4, a) - jnp.where(k > 0.0, SHIFT, 0.0))

    def image_of(get, a):
        n = a + DEPTH - 1
        wl, wh, ws, wz, diag = wa_ref[n], wa_ref[n + 1], ws_ref[n], wz_ref[n], diag_ref[n]
        off = [field(5 + i, a) for i in range(3)]
        u = [get(c, a) for c in range(3)]
        mixed = [off[0] * u[1] + off[1] * u[2], off[0] * u[0] + off[2] * u[2], off[1] * u[0] + off[2] * u[1]]
        out = []
        for c in range(3):
            acc = wh * get(c, a + 1) + wl * get(c, a - 1)
            acc = acc + (ws * turn(u[c], -1, 0) + turn(ws * u[c], 1, 0))
            acc = acc + (wz * turn(u[c], -1, 1) + turn(wz * u[c], 1, 1))
            out.append(diag * u[c] + mixed[c] - acc)
        return out

    for a in range(-2, n_az + 2):
        for c, v in enumerate(image_of(field, a)):
            u1_ref[c, a + 2] = v
    for a in range(-1, n_az + 1):
        for c, v in enumerate(image_of(lambda c, b: u1_ref[c, b + 2], a)):
            u2_ref[c, a + 1] = v
    acc = [jnp.zeros((8, 128), F32) for _ in PAIRS]
    for a in range(n_az):
        for c, v in enumerate(image_of(lambda c, b: u2_ref[c, b + 1], a)):
            v = v[:n_sp]
            u3_ref[c, a] = v
            u = [own[c, a], u1_ref[c, a + 2][:n_sp], u2_ref[c, a + 1][:n_sp], v]
            for n, (i, j) in enumerate(PAIRS):
                acc[n] = acc[n] + folded(u[i] * u[j])
    lane = lax.broadcasted_iota(jnp.int32, (8, 128), 1)
    total = jnp.zeros((8, 128), F32)
    for n in range(len(PAIRS)):
        one = jnp.sum(jnp.sum(acc[n], axis=0, keepdims=True), axis=1, keepdims=True)
        total = jnp.where(lane == n, one, total)
    sums_ref[...] = total


def coefficients(rows):
    lane = lax.broadcasted_iota(jnp.int32, (8, 128), 1)
    row = jnp.broadcast_to(jnp.sum(rows, axis=0, keepdims=True), (8, 128))

    def entry(n):
        return jnp.broadcast_to(jnp.sum(jnp.where(lane == n, row, 0.0), axis=1, keepdims=True), (8, 128))

    g = {p: entry(n) for n, p in enumerate(PAIRS)}
    n0 = g[0, 0]
    m10, m20, m30 = g[0, 1] / n0, g[0, 2] / n0, g[0, 3] / n0
    n1 = g[1, 1] - m10 * g[0, 1]
    t21 = g[1, 2] - m10 * g[0, 2]
    t31 = g[1, 3] - m10 * g[0, 3]
    m21, m31 = t21 / n1, t31 / n1
    n2 = g[2, 2] - m20 * g[0, 2] - m21 * t21
    t32 = g[2, 3] - m20 * g[0, 3] - m21 * t31
    m32 = t32 / n2
    n3 = g[3, 3] - m30 * g[0, 3] - m31 * t31 - m32 * t32
    b0, b1, b2 = SHIFT + m10, SHIFT + m21 - m10, SHIFT + m32 - m21
    g1, g2 = n1 / n0, n2 / n1
    a0 = 1.0 / b0
    a1 = 1.0 / (b1 - g1 * a0)
    a2 = 1.0 / (b2 - g2 * a1)
    safe = jnp.logical_and(
        jnp.logical_and(n1 > SAFE * g[1, 1], n2 > SAFE * g[2, 2]),
        jnp.logical_and(n3 > SAFE * g[3, 3], jnp.logical_and(a1 > 0.0, a2 > 0.0)),
    )
    f = {"m10": m10, "m20": m20, "m21": m21, "m30": m30, "m31": m31, "m32": m32}
    f["e1"], f["e2"] = a0 * g1, a1 * g2
    f["x0"], f["x1"], f["x2"] = a0, -(a0 * a1), a0 * a1 * a2
    f["r3"] = -(a0 * a1 * a2)
    return f, safe


def final_kernel(rows_ref, u0_ref, u1_ref, u2_ref, u3_ref, x_ref, r_ref, safe_ref):
    f, safe = coefficients(rows_ref[...])
    safe_ref[...] = jnp.where(safe, 1.0, 0.0)
    n_az, n_sp, slots = u3_ref.shape[1:]
    f = {key: jnp.concatenate([jnp.concatenate([v] * (n_sp // 8), 0)] * (slots // 128), 1) for key, v in f.items()}
    for c in range(3):
        for a in range(n_az):
            u0, u1, u2, u3 = u0_ref[c, a], u1_ref[c, a + 2][:n_sp], u2_ref[c, a + 1][:n_sp], u3_ref[c, a]
            q1 = u1 - f["m10"] * u0
            q2 = u2 - f["m21"] * q1 - f["m20"] * u0
            q3 = u3 - f["m32"] * q2 - f["m31"] * q1 - f["m30"] * u0
            p1 = q1 - f["e1"] * u0
            p2 = q2 - f["e2"] * p1
            x_ref[c, a] = f["x0"] * u0 + f["x1"] * p1 + f["x2"] * p2
            r_ref[c, a] = f["r3"] * q3


def along_azimuth(lo, hi):
    n = lax.axis_size("azimuth")
    up = [(i, (i + 1) % n) for i in range(n)]
    return lax.ppermute(hi, "azimuth", up), lax.ppermute(lo, "azimuth", [(j, i) for i, j in up])


def along_span(lo, hi):
    up = [(i, i + 1) for i in range(lax.axis_size("span") - 1)]
    return lax.ppermute(hi, "span", up), lax.ppermute(lo, "span", [(j, i) for i, j in up])


def everywhere(row, axis):
    n = lax.axis_size(axis)
    return lax.all_to_all(jnp.broadcast_to(row, (n, 128)), axis, 0, 0, tiled=True)


def on_device(sensitivity, stiffness, spring, shear, interface, live_blocks):
    rows_az, rows_span, slots = stiffness.shape
    blocks = interface.shape[2]
    width = slots // blocks
    field = (3, rows_az, rows_span, slots)
    strip = (4 * DEPTH + 4 * (DEPTH - 1), rows_span, slots)
    tiles = (FIELDS * rows_az, TILE, slots)
    own, lo, hi, sl, sh = call(pack_kernel, [(FIELDS,) + field[1:], strip, strip, tiles, tiles], 6, smem=(0,))(
        live_blocks, sensitivity, stiffness, spring, shear, interface
    )
    ap, an = along_azimuth(lo, hi)
    sp, sn = along_span(sl, sh)
    corner = (5, TILE, slots)
    cp, cn = along_azimuth(*call(corner_kernel, [corner, corner], 2)(sp, sn))
    tall = (rows_span + TILE, slots)
    u1, u2, u3, sums = call(
        basis_kernel,
        [(3, rows_az + 4) + tall, (3, rows_az + 2) + tall, field, (8, 128)],
        7,
        scratch=((rows_az + 5,) + tall,) + ((rows_az + 4,) + tall,) * 3,
    )(own, ap, an, sp, sn, cp, cn)
    sums = jnp.sum(everywhere(sums[0:1], "span"), axis=0, keepdims=True)
    rows = everywhere(sums, "azimuth")
    x, res, safe = call(final_kernel, [field, field, (8, 128)], 5)(rows, own, u1, u2, u3)

    def guarded():
        zpos = lax.broadcasted_iota(jnp.int32, stiffness.shape, 2)
        live = (zpos < live_blocks[0, 0] * width).astype(F32)
        inter = jnp.broadcast_to(interface[:, :, :, None], (rows_az, rows_span, blocks, width))
        inter = inter.reshape(stiffness.shape).astype(F32)
        return stepwise(sensitivity, stiffness, spring, shear, live, inter)

    return lax.cond(safe[0, 0] > 0.5, lambda: (x, res), guarded)


def solution(mesh):
    return jax.shard_map(
        on_device,
        mesh=mesh,
        in_specs=(
            P(None, "azimuth", "span", None),
            P("azimuth", "span", None),
            P("azimuth", "span", None),
            P(None, "azimuth", "span", None),
            P("azimuth", "span", None),
            P("azimuth", "span"),
        ),
        out_specs=(P(None, "azimuth", "span", None), P(None, "azimuth", "span", None)),
        check_vma=False,
    )
```

```python
import functools

import jax
import jax.numpy as jnp
from jax import lax
from jax.experimental import pallas as pl
from jax.experimental.pallas import tpu as pltpu
from jax.sharding import PartitionSpec as P


ITERS = 3
penalty_weight = 4.0
SHIFT = 5.0
SAFE = 0.01
F32 = jnp.float32
VMEM = pl.BlockSpec(memory_space=pltpu.VMEM)
SMEM = pl.BlockSpec(memory_space=pltpu.SMEM)


def padded_2(x, sides, width):
    for axis, dim in sides:
        peers, length = (lax.axis_size(axis), x.shape[dim])
        up = [(i, (i + 1) % peers) for i in range(peers)]
        down = [(j, i) for i, j in up]
        last = lax.slice_in_dim(x, length - width, length, axis=dim)
        leading = lax.slice_in_dim(x, 0, width, axis=dim)
        before = lax.ppermute(last, axis, up)
        after = lax.ppermute(leading, axis, down)
        x = jnp.concatenate([before, x, after], axis=dim)
    return x


def ahead(field, axis):
    count = field.shape[axis]
    rest = lax.slice_in_dim(field, 1, count, axis=axis)
    return jnp.concatenate([rest, jnp.zeros_like(lax.slice_in_dim(field, 0, 1, axis=axis))], axis)


def behind(field, axis):
    count = field.shape[axis]
    rest = lax.slice_in_dim(field, 0, count - 1, axis=axis)
    return jnp.concatenate([jnp.zeros_like(lax.slice_in_dim(field, 0, 1, axis=axis)), rest], axis)


def coupling(field, shear, spring):
    return (
        jnp.stack(
            [
                field[0] + shear[0] * field[1] + shear[1] * field[2],
                shear[0] * field[0] + field[1] + shear[2] * field[2],
                shear[1] * field[0] + shear[2] * field[1] + field[2],
            ]
        )
        * spring
    )


def stepwise(sensitivity, stiffness, spring, shear, live, inter):
    rows_az, rows_span, slots = stiffness.shape
    padded = padded_2(jnp.stack([stiffness, live]), (("azimuth", 1), ("span", 2)), 1)
    kpad = padded[0]
    lpad = padded[1]
    w_ap = live * lpad[2:, 1:-1] * (stiffness + kpad[2:, 1:-1]) * 0.5
    w_am = live * lpad[:-2, 1:-1] * (stiffness + kpad[:-2, 1:-1]) * 0.5
    w_sp = live * lpad[1:-1, 2:] * (stiffness + kpad[1:-1, 2:]) * 0.5
    w_sm = live * lpad[1:-1, :-2] * (stiffness + kpad[1:-1, :-2]) * 0.5
    span_rank = lax.axis_index("span")
    span_count = lax.axis_size("span")
    row = lax.broadcasted_iota(jnp.int32, stiffness.shape, 1)
    top_edge = jnp.logical_and(span_rank == span_count - 1, row == rows_span - 1)
    low_edge = jnp.logical_and(span_rank == 0, row == 0)
    w_sp = jnp.where(top_edge, 0.0, w_sp)
    w_sm = jnp.where(low_edge, 0.0, w_sm)
    w_zp = live * ahead(live, 2) * (stiffness + ahead(stiffness, 2)) * 0.5
    w_zm = live * behind(live, 2) * (stiffness + behind(stiffness, 2)) * 0.5
    residual = live * sensitivity
    solution_field = jnp.zeros_like(residual)

    def squares(vector):
        return lax.psum(jnp.sum(vector * vector), ("azimuth", "span"))

    def iteration(step, carry):
        solution_field, residual, direction, norm_now = carry
        extended = padded_2(direction, (("azimuth", 1), ("span", 2)), 1)
        next_az = extended[:, 2:, 1:-1]
        prev_az = extended[:, :-2, 1:-1]
        next_span = extended[:, 1:-1, 2:]
        prev_span = extended[:, 1:-1, :-2]
        lap = w_ap * (direction - next_az) + w_am * (direction - prev_az)
        lap = lap + w_sp * (direction - next_span) + w_sm * (direction - prev_span)
        lap = (
            lap
            + w_zp * (direction - ahead(direction, 3))
            + w_zm * (direction - behind(direction, 3))
        )
        coupled = coupling(direction, shear, spring)
        image = live * (lap + coupled + penalty_weight * inter * direction)
        alpha = norm_now / lax.psum(jnp.sum(direction * image), ("azimuth", "span"))
        solution_field = solution_field + alpha * direction
        residual = residual - alpha * image
        norm_next = squares(residual)
        direction = residual + norm_next / norm_now * direction
        return solution_field, residual, direction, norm_next

    carry = (solution_field, residual, residual, squares(residual))
    carry = lax.fori_loop(0, ITERS, iteration, carry)
    return carry[0], carry[1]


DEPTH = 3
FIELDS = 8
TILE = 8


def call(kernel, shapes, n_in, smem=(), scratch=()):
    return pl.pallas_call(
        kernel,
        out_shape=[jax.ShapeDtypeStruct(s, F32) for s in shapes],
        in_specs=[SMEM if i in smem else VMEM for i in range(n_in)],
        out_specs=[VMEM] * len(shapes),
        scratch_shapes=[pltpu.VMEM(s, F32) for s in scratch],
        compiler_params=pltpu.CompilerParams(vmem_limit_bytes=32 << 20),
    )


def reach(f):
    return DEPTH if f < 4 else DEPTH - 1


def place(f, d):
    return 2 * (f * DEPTH + d - 1 if f < 4 else 4 * DEPTH + (f - 4) * (DEPTH - 1) + d - 1)


STRIP = 2 * (4 * DEPTH + 4 * (DEPTH - 1))
CORNER = 5


def sublane(slots):
    return lax.broadcasted_iota(jnp.int32, (TILE, slots), 0)


def turn(x, shift, axis):
    shift = shift % x.shape[axis]
    return pltpu.roll(x, shift, axis) if shift else x


def packed_rows(tiles, sign):
    s = sublane(tiles[0].shape[1])
    s = s if sign > 0 else TILE - 1 - s
    out = [jnp.where(s < 3, tiles[f], turn(tiles[f + 1], sign * 3, 0)) for f in (0, 2)]
    last = tiles[4]
    for j in range(1, 4):
        last = jnp.where(s < 2 * j, last, turn(tiles[4 + j], sign * 2 * j, 0))
    return out + [last]


def unpacked(ref, f, a, sign):
    tile = ref[3 * a + (f // 2 if f < 4 else 2)]
    return turn(tile, -sign * (3 * (f % 2) if f < 4 else 2 * (f - 4)), 0)


def pack_kernel(blocks_ref, s_ref, k_ref, spring_ref, shear_ref, inter_ref, own_ref, sl_ref, sh_ref):
    n_az, n_sp, slots = k_ref.shape
    blocks = inter_ref.shape[1]
    width = slots // blocks
    zpos = lax.broadcasted_iota(jnp.int32, (n_sp, slots), 1)
    live = zpos < jnp.broadcast_to(blocks_ref[...] * width, (n_sp, slots))
    same = lax.broadcasted_iota(jnp.int32, (n_sp, n_sp), 0) == lax.broadcasted_iota(jnp.int32, (n_sp, n_sp), 1)
    for a in range(n_az):
        spring = spring_ref[a]
        flags = inter_ref[a].astype(F32)
        columns = []
        for b in range(blocks):
            row = jnp.broadcast_to(flags[b : b + 1, :], (n_sp, n_sp))
            column = jnp.sum(jnp.where(same, row, 0.0), axis=1, keepdims=True)
            columns.append(jnp.broadcast_to(column, (n_sp, width)))
        inter = jnp.concatenate(columns, axis=1)
        fields = [s_ref[c, a] for c in range(3)] + [k_ref[a], spring + penalty_weight * inter]
        fields += [shear_ref[i, a] * spring for i in range(3)]
        fields = [jnp.where(live, v, 0.0) for v in fields]
        for f, v in enumerate(fields):
            own_ref[f, a] = v
        for n, v in enumerate(packed_rows([v[:TILE] for v in fields], 1)):
            sl_ref[3 * a + n] = v
        for n, v in enumerate(packed_rows([v[n_sp - TILE :] for v in fields], -1)):
            sh_ref[3 * a + n] = v


def side_kernel(own_ref, sp_ref, sn_ref, lo_ref, hi_ref, near_ref):
    n_az = own_ref.shape[1]
    s = sublane(own_ref.shape[3])
    tiles = {}
    for a in range(n_az):
        for f in range(FIELDS):
            tile = jnp.where(s < TILE // 2, unpacked(sn_ref, f, a, 1), unpacked(sp_ref, f, a, -1))
            near_ref[f * n_az + a] = tile
            tiles[f, a] = tile
    for out, one, step in ((lo_ref, 0, 1), (hi_ref, n_az - 1, -1)):
        for f in range(FIELDS):
            for d in range(1, reach(f) + 1):
                v = own_ref[f, one + step * (d - 1)]
                out[place(f, d)] = v[:TILE]
                out[place(f, d) + 1] = v[TILE:]
        for f in range(4):
            far = tiles[f, one + step]
            out[STRIP + f] = jnp.where(
                s == 2, turn(far, 2, 0), jnp.where(s == TILE - 3, turn(far, -2, 0), tiles[f, one])
            )
        packed = tiles[4, one]
        for j in range(1, 4):
            v = tiles[4 + j, one]
            packed = jnp.where(s == j, turn(v, j, 0), jnp.where(s == TILE - 1 - j, turn(v, -j, 0), packed))
        out[STRIP + 4] = packed


PAIRS = ((0, 0), (0, 1), (0, 2), (0, 3), (1, 1), (1, 2), (1, 3), (2, 2), (2, 3), (3, 3))


def folded(x):
    n, m = x.shape
    x = x.reshape(n // 8, 8, m).sum(0) if n > 8 else x
    out = x[:, 0:128]
    for b in range(1, m // 128):
        out = out + x[:, b * 128 : (b + 1) * 128]
    return out


def basis_kernel(own, near, ap, an, u1_ref, u2_ref, u3_ref, sums_ref, wa_ref, ws_ref, wz_ref, diag_ref):
    n_az, n_sp, slots = own.shape[1:]
    s = sublane(slots)
    lane = lax.broadcasted_iota(jnp.int32, (n_sp + TILE, slots), 1)

    def field(f, a):
        if 0 <= a < n_az:
            return jnp.concatenate([own[f, a], near[f * n_az + a]], axis=0)
        side, d = (an, a - n_az + 1) if a >= n_az else (ap, -a)
        if f < 4:
            tile = side[STRIP + f]
            if d == 2:
                tile = jnp.where(s < TILE // 2, turn(tile, -2, 0), turn(tile, 2, 0))
        else:
            j = f - 4
            tile = side[STRIP + 4]
            tile = jnp.where(s < TILE // 2, turn(tile, -j, 0), turn(tile, j, 0))
        return jnp.concatenate([side[place(f, d)], side[place(f, d) + 1], tile], axis=0)

    def face(k, near):
        return jnp.where(jnp.minimum(k, near) > 0.0, (k + near) * 0.5, 0.0)

    for a in range(-DEPTH, n_az + DEPTH - 1):
        wa_ref[a + DEPTH] = face(field(3, a), field(3, a + 1))
    for a in range(1 - DEPTH, n_az + DEPTH - 1):
        k = field(3, a)
        ws = face(k, turn(k, -1, 0))
        wz = face(k, jnp.where(lane == slots - 1, 0.0, turn(k, -1, 1)))
        n = a + DEPTH - 1
        ws_ref[n], wz_ref[n] = ws, wz
        total = (wa_ref[n] + wa_ref[n + 1]) + (ws + turn(ws, 1, 0)) + (wz + turn(wz, 1, 1))
        diag_ref[n] = total + (field(4, a) - jnp.where(k > 0.0, SHIFT, 0.0))

    def image_of(get, a):
        n = a + DEPTH - 1
        wl, wh, ws, wz, diag = wa_ref[n], wa_ref[n + 1], ws_ref[n], wz_ref[n], diag_ref[n]
        off = [field(5 + i, a) for i in range(3)]
        u = [get(c, a) for c in range(3)]
        mixed = [off[0] * u[1] + off[1] * u[2], off[0] * u[0] + off[2] * u[2], off[1] * u[0] + off[2] * u[1]]
        out = []
        for c in range(3):
            acc = wh * get(c, a + 1) + wl * get(c, a - 1)
            acc = acc + (ws * turn(u[c], -1, 0) + turn(ws * u[c], 1, 0))
            acc = acc + (wz * turn(u[c], -1, 1) + turn(wz * u[c], 1, 1))
            out.append(diag * u[c] + mixed[c] - acc)
        return out

    for a in range(-2, n_az + 2):
        for c, v in enumerate(image_of(field, a)):
            u1_ref[c, a + 2] = v
    for a in range(-1, n_az + 1):
        for c, v in enumerate(image_of(lambda c, b: u1_ref[c, b + 2], a)):
            u2_ref[c, a + 1] = v
    acc = [jnp.zeros((8, 128), F32) for _ in PAIRS]
    for a in range(n_az):
        for c, v in enumerate(image_of(lambda c, b: u2_ref[c, b + 1], a)):
            v = v[:n_sp]
            u3_ref[c, a] = v
            u = [own[c, a], u1_ref[c, a + 2][:n_sp], u2_ref[c, a + 1][:n_sp], v]
            for n, (i, j) in enumerate(PAIRS):
                acc[n] = acc[n] + folded(u[i] * u[j])
    lane = lax.broadcasted_iota(jnp.int32, (8, 128), 1)
    total = jnp.zeros((8, 128), F32)
    for n in range(len(PAIRS)):
        one = jnp.sum(jnp.sum(acc[n], axis=0, keepdims=True), axis=1, keepdims=True)
        total = jnp.where(lane == n, one, total)
    sums_ref[...] = total


def coefficients(rows):
    lane = lax.broadcasted_iota(jnp.int32, (8, 128), 1)
    row = jnp.broadcast_to(jnp.sum(rows, axis=0, keepdims=True), (8, 128))

    def entry(n):
        return jnp.broadcast_to(jnp.sum(jnp.where(lane == n, row, 0.0), axis=1, keepdims=True), (8, 128))

    g = {p: entry(n) for n, p in enumerate(PAIRS)}
    n0 = g[0, 0]
    m10, m20, m30 = g[0, 1] / n0, g[0, 2] / n0, g[0, 3] / n0
    n1 = g[1, 1] - m10 * g[0, 1]
    t21 = g[1, 2] - m10 * g[0, 2]
    t31 = g[1, 3] - m10 * g[0, 3]
    m21, m31 = t21 / n1, t31 / n1
    n2 = g[2, 2] - m20 * g[0, 2] - m21 * t21
    t32 = g[2, 3] - m20 * g[0, 3] - m21 * t31
    m32 = t32 / n2
    n3 = g[3, 3] - m30 * g[0, 3] - m31 * t31 - m32 * t32
    b0, b1, b2 = SHIFT + m10, SHIFT + m21 - m10, SHIFT + m32 - m21
    g1, g2 = n1 / n0, n2 / n1
    a0 = 1.0 / b0
    a1 = 1.0 / (b1 - g1 * a0)
    a2 = 1.0 / (b2 - g2 * a1)
    safe = jnp.logical_and(
        jnp.logical_and(n1 > SAFE * g[1, 1], n2 > SAFE * g[2, 2]),
        jnp.logical_and(n3 > SAFE * g[3, 3], jnp.logical_and(a1 > 0.0, a2 > 0.0)),
    )
    f = {"m10": m10, "m20": m20, "m21": m21, "m30": m30, "m31": m31, "m32": m32}
    f["e1"], f["e2"] = a0 * g1, a1 * g2
    f["x0"], f["x1"], f["x2"] = a0, -(a0 * a1), a0 * a1 * a2
    f["r3"] = -(a0 * a1 * a2)
    return f, safe


def final_kernel(rows_ref, u0_ref, u1_ref, u2_ref, u3_ref, x_ref, r_ref, safe_ref):
    f, safe = coefficients(rows_ref[...])
    safe_ref[...] = jnp.where(safe, 1.0, 0.0)[0:1, 0:1]
    n_az, n_sp, slots = u3_ref.shape[1:]
    f = {key: jnp.concatenate([jnp.concatenate([v] * (n_sp // 8), 0)] * (slots // 128), 1) for key, v in f.items()}
    for c in range(3):
        for a in range(n_az):
            u0, u1, u2, u3 = u0_ref[c, a], u1_ref[c, a + 2][:n_sp], u2_ref[c, a + 1][:n_sp], u3_ref[c, a]
            q1 = u1 - f["m10"] * u0
            q2 = u2 - f["m21"] * q1 - f["m20"] * u0
            q3 = u3 - f["m32"] * q2 - f["m31"] * q1 - f["m30"] * u0
            p1 = q1 - f["e1"] * u0
            p2 = q2 - f["e2"] * p1
            x_ref[c, a] = f["x0"] * u0 + f["x1"] * p1 + f["x2"] * p2
            r_ref[c, a] = f["r3"] * q3


def along_azimuth(lo, hi):
    n = lax.axis_size("azimuth")
    up = [(i, (i + 1) % n) for i in range(n)]
    return lax.ppermute(hi, "azimuth", up), lax.ppermute(lo, "azimuth", [(j, i) for i, j in up])


def along_span(lo, hi):
    up = [(i, i + 1) for i in range(lax.axis_size("span") - 1)]
    return lax.ppermute(hi, "span", up), lax.ppermute(lo, "span", [(j, i) for i, j in up])


def everywhere(row, axis):
    n = lax.axis_size(axis)
    return lax.all_to_all(jnp.broadcast_to(row, (n, 128)), axis, 0, 0, tiled=True)


def on_device(sensitivity, stiffness, spring, shear, interface, live_blocks):
    rows_az, rows_span, slots = stiffness.shape
    blocks = interface.shape[2]
    width = slots // blocks
    field = (3, rows_az, rows_span, slots)
    tiles = (3 * rows_az, TILE, slots)
    own, sl, sh = call(pack_kernel, [(FIELDS,) + field[1:], tiles, tiles], 6)(
        live_blocks, sensitivity, stiffness, spring, shear, jnp.transpose(interface, (0, 2, 1))
    )
    sp, sn = along_span(sl, sh)
    strip = (STRIP + CORNER, TILE, slots)
    lo, hi, near = call(side_kernel, [strip, strip, (FIELDS * rows_az, TILE, slots)], 3)(own, sp, sn)
    ap, an = along_azimuth(lo, hi)
    tall = (rows_span + TILE, slots)
    u1, u2, u3, sums = call(
        basis_kernel,
        [(3, rows_az + 4) + tall, (3, rows_az + 2) + tall, field, (8, 128)],
        4,
        scratch=((rows_az + 5,) + tall,) + ((rows_az + 4,) + tall,) * 3,
    )(own, near, ap, an)
    sums = jnp.sum(everywhere(sums[0:1], "span"), axis=0, keepdims=True)
    rows = everywhere(sums, "azimuth")
    rows, sensitivity, stiffness, spring, shear, interface, live_blocks = lax.optimization_barrier(
        (rows, sensitivity, stiffness, spring, shear, interface, live_blocks)
    )
    x, res, safe = call(final_kernel, [field, field, (1, 1)], 5)(rows, own, u1, u2, u3)

    def guarded():
        zpos = lax.broadcasted_iota(jnp.int32, stiffness.shape, 2)
        live = (zpos < live_blocks[0, 0] * width).astype(F32)
        inter = jnp.broadcast_to(interface[:, :, :, None], (rows_az, rows_span, blocks, width))
        inter = inter.reshape(stiffness.shape).astype(F32)
        return stepwise(sensitivity, stiffness, spring, shear, live, inter)

    return lax.cond(safe[0, 0] > 0.5, lambda: (x, res), guarded)


def solution(mesh):
    return jax.shard_map(
        on_device,
        mesh=mesh,
        in_specs=(
            P(None, "azimuth", "span", None),
            P("azimuth", "span", None),
            P("azimuth", "span", None),
            P(None, "azimuth", "span", None),
            P("azimuth", "span", None),
            P("azimuth", "span"),
        ),
        out_specs=(P(None, "azimuth", "span", None), P(None, "azimuth", "span", None)),
        check_vma=False,
    )
```

```python
import functools

import jax
import jax.numpy as jnp
from jax import lax
from jax.experimental import pallas as pl
from jax.experimental.pallas import tpu as pltpu
from jax.sharding import PartitionSpec as P


ITERS = 3
penalty_weight = 4.0
SHIFT = 5.0
SAFE = 0.01
F32 = jnp.float32
VMEM = pl.BlockSpec(memory_space=pltpu.VMEM)
SMEM = pl.BlockSpec(memory_space=pltpu.SMEM)


def padded_2(x, sides, width):
    for axis, dim in sides:
        peers, length = (lax.axis_size(axis), x.shape[dim])
        up = [(i, (i + 1) % peers) for i in range(peers)]
        down = [(j, i) for i, j in up]
        last = lax.slice_in_dim(x, length - width, length, axis=dim)
        leading = lax.slice_in_dim(x, 0, width, axis=dim)
        before = lax.ppermute(last, axis, up)
        after = lax.ppermute(leading, axis, down)
        x = jnp.concatenate([before, x, after], axis=dim)
    return x


def ahead(field, axis):
    count = field.shape[axis]
    rest = lax.slice_in_dim(field, 1, count, axis=axis)
    return jnp.concatenate([rest, jnp.zeros_like(lax.slice_in_dim(field, 0, 1, axis=axis))], axis)


def behind(field, axis):
    count = field.shape[axis]
    rest = lax.slice_in_dim(field, 0, count - 1, axis=axis)
    return jnp.concatenate([jnp.zeros_like(lax.slice_in_dim(field, 0, 1, axis=axis)), rest], axis)


def coupling(field, shear, spring):
    return (
        jnp.stack(
            [
                field[0] + shear[0] * field[1] + shear[1] * field[2],
                shear[0] * field[0] + field[1] + shear[2] * field[2],
                shear[1] * field[0] + shear[2] * field[1] + field[2],
            ]
        )
        * spring
    )


def stepwise(sensitivity, stiffness, spring, shear, live, inter):
    rows_az, rows_span, slots = stiffness.shape
    padded = padded_2(jnp.stack([stiffness, live]), (("azimuth", 1), ("span", 2)), 1)
    kpad = padded[0]
    lpad = padded[1]
    w_ap = live * lpad[2:, 1:-1] * (stiffness + kpad[2:, 1:-1]) * 0.5
    w_am = live * lpad[:-2, 1:-1] * (stiffness + kpad[:-2, 1:-1]) * 0.5
    w_sp = live * lpad[1:-1, 2:] * (stiffness + kpad[1:-1, 2:]) * 0.5
    w_sm = live * lpad[1:-1, :-2] * (stiffness + kpad[1:-1, :-2]) * 0.5
    span_rank = lax.axis_index("span")
    span_count = lax.axis_size("span")
    row = lax.broadcasted_iota(jnp.int32, stiffness.shape, 1)
    top_edge = jnp.logical_and(span_rank == span_count - 1, row == rows_span - 1)
    low_edge = jnp.logical_and(span_rank == 0, row == 0)
    w_sp = jnp.where(top_edge, 0.0, w_sp)
    w_sm = jnp.where(low_edge, 0.0, w_sm)
    w_zp = live * ahead(live, 2) * (stiffness + ahead(stiffness, 2)) * 0.5
    w_zm = live * behind(live, 2) * (stiffness + behind(stiffness, 2)) * 0.5
    residual = live * sensitivity
    solution_field = jnp.zeros_like(residual)

    def squares(vector):
        return lax.psum(jnp.sum(vector * vector), ("azimuth", "span"))

    def iteration(step, carry):
        solution_field, residual, direction, norm_now = carry
        extended = padded_2(direction, (("azimuth", 1), ("span", 2)), 1)
        next_az = extended[:, 2:, 1:-1]
        prev_az = extended[:, :-2, 1:-1]
        next_span = extended[:, 1:-1, 2:]
        prev_span = extended[:, 1:-1, :-2]
        lap = w_ap * (direction - next_az) + w_am * (direction - prev_az)
        lap = lap + w_sp * (direction - next_span) + w_sm * (direction - prev_span)
        lap = (
            lap
            + w_zp * (direction - ahead(direction, 3))
            + w_zm * (direction - behind(direction, 3))
        )
        coupled = coupling(direction, shear, spring)
        image = live * (lap + coupled + penalty_weight * inter * direction)
        alpha = norm_now / lax.psum(jnp.sum(direction * image), ("azimuth", "span"))
        solution_field = solution_field + alpha * direction
        residual = residual - alpha * image
        norm_next = squares(residual)
        direction = residual + norm_next / norm_now * direction
        return solution_field, residual, direction, norm_next

    carry = (solution_field, residual, residual, squares(residual))
    carry = lax.fori_loop(0, ITERS, iteration, carry)
    return carry[0], carry[1]


DEPTH = 3
FIELDS = 8
TILE = 8


def call(kernel, shapes, n_in, smem=(), scratch=()):
    return pl.pallas_call(
        kernel,
        out_shape=[jax.ShapeDtypeStruct(s, F32) for s in shapes],
        in_specs=[SMEM if i in smem else VMEM for i in range(n_in)],
        out_specs=[VMEM] * len(shapes),
        scratch_shapes=[pltpu.VMEM(s, F32) for s in scratch],
        compiler_params=pltpu.CompilerParams(vmem_limit_bytes=32 << 20),
    )


def reach(f):
    return DEPTH if f < 4 else DEPTH - 1


def place(f, d):
    return f * DEPTH + d - 1 if f < 4 else 4 * DEPTH + (f - 4) * (DEPTH - 1) + d - 1


STRIP = 4 * DEPTH + 4 * (DEPTH - 1)
CORNER = 5


def even(axis):
    return lax.axis_index(axis) % 2 == 0


def sublane(slots):
    return lax.broadcasted_iota(jnp.int32, (TILE, slots), 0)


def turn(x, shift, axis):
    shift = shift % x.shape[axis]
    return pltpu.roll(x, shift, axis) if shift else x


def packed_rows(tiles, sign):
    s = sublane(tiles[0].shape[1])
    s = s if sign > 0 else TILE - 1 - s
    out = [jnp.where(s < 3, tiles[f], turn(tiles[f + 1], sign * 3, 0)) for f in (0, 2)]
    last = tiles[4]
    for j in range(1, 4):
        last = jnp.where(s < 2 * j, last, turn(tiles[4 + j], sign * 2 * j, 0))
    return out + [last]


def unpacked(ref, f, a, sign):
    tile = ref[3 * a + (f // 2 if f < 4 else 2)]
    return turn(tile, -sign * (3 * (f % 2) if f < 4 else 2 * (f - 4)), 0)


def pack_kernel(blocks_ref, s_ref, k_ref, spring_ref, shear_ref, inter_ref, own_ref, me_ref, mo_ref, se_ref, so_ref):
    n_az, n_sp, slots = k_ref.shape
    blocks = inter_ref.shape[1]
    width = slots // blocks
    zpos = lax.broadcasted_iota(jnp.int32, (n_sp, slots), 1)
    live = zpos < jnp.broadcast_to(blocks_ref[...] * width, (n_sp, slots))
    same = lax.broadcasted_iota(jnp.int32, (n_sp, n_sp), 0) == lax.broadcasted_iota(jnp.int32, (n_sp, n_sp), 1)
    for a in range(n_az):
        spring = spring_ref[a]
        flags = inter_ref[a].astype(F32)
        columns = []
        for b in range(blocks):
            row = jnp.broadcast_to(flags[b : b + 1, :], (n_sp, n_sp))
            column = jnp.sum(jnp.where(same, row, 0.0), axis=1, keepdims=True)
            columns.append(jnp.broadcast_to(column, (n_sp, width)))
        inter = jnp.concatenate(columns, axis=1)
        fields = [s_ref[c, a] for c in range(3)] + [k_ref[a], spring + penalty_weight * inter]
        fields += [shear_ref[i, a] * spring for i in range(3)]
        fields = [jnp.where(live, v, 0.0) for v in fields]
        for f, v in enumerate(fields):
            own_ref[f, a] = v
        first = packed_rows([v[:TILE] for v in fields], 1)
        last = packed_rows([v[n_sp - TILE :] for v in fields], -1)
        up = even("span")
        for n in range(3):
            se_ref[3 * a + n] = jnp.where(up, last[n], first[n])
            so_ref[3 * a + n] = jnp.where(up, first[n], last[n])
    flip = even("azimuth")
    for f in range(FIELDS):
        for d in range(1, reach(f) + 1):
            me_ref[place(f, d)] = own_ref[f, jnp.where(flip, n_az - d, d - 1)]
            mo_ref[place(f, d)] = own_ref[f, jnp.where(flip, d - 1, n_az - d)]


def side_kernel(se_ref, so_ref, near_ref, ce_ref, co_ref):
    n_az = se_ref.shape[0] // 3
    s = sublane(se_ref.shape[2])
    up, flip = even("span"), even("azimuth")
    after = [jnp.where(up, se_ref[n], so_ref[n]) for n in range(3 * n_az)]
    before = [jnp.where(up, so_ref[n], se_ref[n]) for n in range(3 * n_az)]
    tiles = {}
    for a in range(n_az):
        for f in range(FIELDS):
            tile = jnp.where(s < TILE // 2, unpacked(after, f, a, 1), unpacked(before, f, a, -1))
            near_ref[f * n_az + a] = tile
            tiles[f, a] = tile

    def corner(one, step):
        out = []
        for f in range(4):
            far = tiles[f, one + step]
            out.append(
                jnp.where(s == 2, turn(far, 2, 0), jnp.where(s == TILE - 3, turn(far, -2, 0), tiles[f, one]))
            )
        packed = tiles[4, one]
        for j in range(1, 4):
            v = tiles[4 + j, one]
            packed = jnp.where(s == j, turn(v, j, 0), jnp.where(s == TILE - 1 - j, turn(v, -j, 0), packed))
        return out + [packed]

    for n, (low, high) in enumerate(zip(corner(0, 1), corner(n_az - 1, -1))):
        ce_ref[n] = jnp.where(flip, high, low)
        co_ref[n] = jnp.where(flip, low, high)


PAIRS = ((0, 0), (0, 1), (0, 2), (0, 3), (1, 1), (1, 2), (1, 3), (2, 2), (2, 3), (3, 3))


def folded(x):
    n, m = x.shape
    x = x.reshape(n // 8, 8, m).sum(0) if n > 8 else x
    out = x[:, 0:128]
    for b in range(1, m // 128):
        out = out + x[:, b * 128 : (b + 1) * 128]
    return out


def basis_kernel(own, near, me, mo, ce, co, *rest):
    flip = even("azimuth")

    @pl.when(flip)
    def _():
        basis(own, near, (mo, co), (me, ce), *rest)

    @pl.when(jnp.logical_not(flip))
    def _():
        basis(own, near, (me, ce), (mo, co), *rest)


def basis(own, near, low, high, u1_ref, u2_ref, u3_ref, sums_ref, wa_ref, ws_ref, wz_ref, diag_ref):
    n_az, n_sp, slots = own.shape[1:]
    s = sublane(slots)
    lane = lax.broadcasted_iota(jnp.int32, (n_sp + TILE, slots), 1)

    def field(f, a):
        if 0 <= a < n_az:
            return jnp.concatenate([own[f, a], near[f * n_az + a]], axis=0)
        (side, corner), d = (high, a - n_az + 1) if a >= n_az else (low, -a)
        if f < 4:
            tile = corner[f]
            if d == 2:
                tile = jnp.where(s < TILE // 2, turn(tile, -2, 0), turn(tile, 2, 0))
        else:
            j = f - 4
            tile = corner[4]
            tile = jnp.where(s < TILE // 2, turn(tile, -j, 0), turn(tile, j, 0))
        return jnp.concatenate([side[place(f, d)], tile], axis=0)

    def face(k, near):
        return jnp.where(jnp.minimum(k, near) > 0.0, (k + near) * 0.5, 0.0)

    for a in range(-DEPTH, n_az + DEPTH - 1):
        wa_ref[a + DEPTH] = face(field(3, a), field(3, a + 1))
    for a in range(1 - DEPTH, n_az + DEPTH - 1):
        k = field(3, a)
        ws = face(k, turn(k, -1, 0))
        wz = face(k, jnp.where(lane == slots - 1, 0.0, turn(k, -1, 1)))
        n = a + DEPTH - 1
        ws_ref[n], wz_ref[n] = ws, wz
        total = (wa_ref[n] + wa_ref[n + 1]) + (ws + turn(ws, 1, 0)) + (wz + turn(wz, 1, 1))
        diag_ref[n] = total + (field(4, a) - jnp.where(k > 0.0, SHIFT, 0.0))

    def image_of(get, a):
        n = a + DEPTH - 1
        wl, wh, ws, wz, diag = wa_ref[n], wa_ref[n + 1], ws_ref[n], wz_ref[n], diag_ref[n]
        off = [field(5 + i, a) for i in range(3)]
        u = [get(c, a) for c in range(3)]
        mixed = [off[0] * u[1] + off[1] * u[2], off[0] * u[0] + off[2] * u[2], off[1] * u[0] + off[2] * u[1]]
        out = []
        for c in range(3):
            acc = wh * get(c, a + 1) + wl * get(c, a - 1)
            acc = acc + (ws * turn(u[c], -1, 0) + turn(ws * u[c], 1, 0))
            acc = acc + (wz * turn(u[c], -1, 1) + turn(wz * u[c], 1, 1))
            out.append(diag * u[c] + mixed[c] - acc)
        return out

    for a in range(-2, n_az + 2):
        for c, v in enumerate(image_of(field, a)):
            u1_ref[c, a + 2] = v
    for a in range(-1, n_az + 1):
        for c, v in enumerate(image_of(lambda c, b: u1_ref[c, b + 2], a)):
            u2_ref[c, a + 1] = v
    acc = [jnp.zeros((8, 128), F32) for _ in PAIRS]
    for a in range(n_az):
        for c, v in enumerate(image_of(lambda c, b: u2_ref[c, b + 1], a)):
            v = v[:n_sp]
            u3_ref[c, a] = v
            u = [own[c, a], u1_ref[c, a + 2][:n_sp], u2_ref[c, a + 1][:n_sp], v]
            for n, (i, j) in enumerate(PAIRS):
                acc[n] = acc[n] + folded(u[i] * u[j])
    lane = lax.broadcasted_iota(jnp.int32, (8, 128), 1)
    total = jnp.zeros((8, 128), F32)
    for n in range(len(PAIRS)):
        one = jnp.sum(jnp.sum(acc[n], axis=0, keepdims=True), axis=1, keepdims=True)
        total = jnp.where(lane == n, one, total)
    sums_ref[...] = total


def coefficients(rows):
    lane = lax.broadcasted_iota(jnp.int32, (8, 128), 1)
    row = jnp.broadcast_to(jnp.sum(rows, axis=0, keepdims=True), (8, 128))

    def entry(n):
        return jnp.broadcast_to(jnp.sum(jnp.where(lane == n, row, 0.0), axis=1, keepdims=True), (8, 128))

    g = {p: entry(n) for n, p in enumerate(PAIRS)}
    n0 = g[0, 0]
    m10, m20, m30 = g[0, 1] / n0, g[0, 2] / n0, g[0, 3] / n0
    n1 = g[1, 1] - m10 * g[0, 1]
    t21 = g[1, 2] - m10 * g[0, 2]
    t31 = g[1, 3] - m10 * g[0, 3]
    m21, m31 = t21 / n1, t31 / n1
    n2 = g[2, 2] - m20 * g[0, 2] - m21 * t21
    t32 = g[2, 3] - m20 * g[0, 3] - m21 * t31
    m32 = t32 / n2
    n3 = g[3, 3] - m30 * g[0, 3] - m31 * t31 - m32 * t32
    b0, b1, b2 = SHIFT + m10, SHIFT + m21 - m10, SHIFT + m32 - m21
    g1, g2 = n1 / n0, n2 / n1
    a0 = 1.0 / b0
    a1 = 1.0 / (b1 - g1 * a0)
    a2 = 1.0 / (b2 - g2 * a1)
    safe = jnp.logical_and(
        jnp.logical_and(n1 > SAFE * g[1, 1], n2 > SAFE * g[2, 2]),
        jnp.logical_and(n3 > SAFE * g[3, 3], jnp.logical_and(a1 > 0.0, a2 > 0.0)),
    )
    f = {"m10": m10, "m20": m20, "m21": m21, "m30": m30, "m31": m31, "m32": m32}
    f["e1"], f["e2"] = a0 * g1, a1 * g2
    f["x0"], f["x1"], f["x2"] = a0, -(a0 * a1), a0 * a1 * a2
    f["r3"] = -(a0 * a1 * a2)
    return f, safe


def final_kernel(rows_ref, u0_ref, u1_ref, u2_ref, u3_ref, x_ref, r_ref, safe_ref):
    f, safe = coefficients(rows_ref[...])
    safe_ref[...] = jnp.where(safe, 1.0, 0.0)[0:1, 0:1]
    n_az, n_sp, slots = u3_ref.shape[1:]
    f = {key: jnp.concatenate([jnp.concatenate([v] * (n_sp // 8), 0)] * (slots // 128), 1) for key, v in f.items()}
    for c in range(3):
        for a in range(n_az):
            u0, u1, u2, u3 = u0_ref[c, a], u1_ref[c, a + 2][:n_sp], u2_ref[c, a + 1][:n_sp], u3_ref[c, a]
            q1 = u1 - f["m10"] * u0
            q2 = u2 - f["m21"] * q1 - f["m20"] * u0
            q3 = u3 - f["m32"] * q2 - f["m31"] * q1 - f["m30"] * u0
            p1 = q1 - f["e1"] * u0
            p2 = q2 - f["e2"] * p1
            x_ref[c, a] = f["x0"] * u0 + f["x1"] * p1 + f["x2"] * p2
            r_ref[c, a] = f["r3"] * q3


def swaps(evens, odds, axis, wraps):
    n = lax.axis_size(axis)
    first = [(i, i + 1) for i in range(0, n, 2)]
    second = [(i, (i + 1) % n) for i in range(1, n if wraps else n - 1, 2)]
    return [
        lax.ppermute(v, axis, pairs + [(j, i) for i, j in pairs]) for v, pairs in ((evens, first), (odds, second))
    ]


def everywhere(row, axis):
    n = lax.axis_size(axis)
    return lax.all_to_all(jnp.broadcast_to(row, (n, 128)), axis, 0, 0, tiled=True)


def on_device(sensitivity, stiffness, spring, shear, interface, live_blocks):
    rows_az, rows_span, slots = stiffness.shape
    blocks = interface.shape[2]
    width = slots // blocks
    field = (3, rows_az, rows_span, slots)
    strip = (STRIP, rows_span, slots)
    tiles = (3 * rows_az, TILE, slots)
    own, me, mo, se, so = call(pack_kernel, [(FIELDS,) + field[1:], strip, strip, tiles, tiles], 6)(
        live_blocks, sensitivity, stiffness, spring, shear, jnp.transpose(interface, (0, 2, 1))
    )
    se, so = swaps(se, so, "span", False)
    me, mo = swaps(me, mo, "azimuth", True)
    corner = (CORNER, TILE, slots)
    near, ce, co = call(side_kernel, [(FIELDS * rows_az, TILE, slots), corner, corner], 2)(se, so)
    ce, co = swaps(ce, co, "azimuth", True)
    tall = (rows_span + TILE, slots)
    u1, u2, u3, sums = call(
        basis_kernel,
        [(3, rows_az + 4) + tall, (3, rows_az + 2) + tall, field, (8, 128)],
        6,
        scratch=((rows_az + 5,) + tall,) + ((rows_az + 4,) + tall,) * 3,
    )(own, near, me, mo, ce, co)
    sums = jnp.sum(everywhere(sums[0:1], "span"), axis=0, keepdims=True)
    rows = everywhere(sums, "azimuth")
    rows, sensitivity, stiffness, spring, shear, interface, live_blocks = lax.optimization_barrier(
        (rows, sensitivity, stiffness, spring, shear, interface, live_blocks)
    )
    x, res, safe = call(final_kernel, [field, field, (1, 1)], 5)(rows, own, u1, u2, u3)

    def guarded():
        zpos = lax.broadcasted_iota(jnp.int32, stiffness.shape, 2)
        live = (zpos < live_blocks[0, 0] * width).astype(F32)
        inter = jnp.broadcast_to(interface[:, :, :, None], (rows_az, rows_span, blocks, width))
        inter = inter.reshape(stiffness.shape).astype(F32)
        return stepwise(sensitivity, stiffness, spring, shear, live, inter)

    return lax.cond(safe[0, 0] > 0.5, lambda: (x, res), guarded)


def solution(mesh):
    return jax.shard_map(
        on_device,
        mesh=mesh,
        in_specs=(
            P(None, "azimuth", "span", None),
            P("azimuth", "span", None),
            P("azimuth", "span", None),
            P(None, "azimuth", "span", None),
            P("azimuth", "span", None),
            P("azimuth", "span"),
        ),
        out_specs=(P(None, "azimuth", "span", None), P(None, "azimuth", "span", None)),
        check_vma=False,
    )
```

```python
import functools

import jax
import jax.numpy as jnp
from jax import lax
from jax.experimental import pallas as pl
from jax.experimental.pallas import tpu as pltpu
from jax.sharding import PartitionSpec as P


ITERS = 3
penalty_weight = 4.0
SHIFT = 5.0
SAFE = 0.01
F32 = jnp.float32
VMEM = pl.BlockSpec(memory_space=pltpu.VMEM)
SMEM = pl.BlockSpec(memory_space=pltpu.SMEM)


def padded_2(x, sides, width):
    for axis, dim in sides:
        peers, length = (lax.axis_size(axis), x.shape[dim])
        up = [(i, (i + 1) % peers) for i in range(peers)]
        down = [(j, i) for i, j in up]
        last = lax.slice_in_dim(x, length - width, length, axis=dim)
        leading = lax.slice_in_dim(x, 0, width, axis=dim)
        before = lax.ppermute(last, axis, up)
        after = lax.ppermute(leading, axis, down)
        x = jnp.concatenate([before, x, after], axis=dim)
    return x


def ahead(field, axis):
    count = field.shape[axis]
    rest = lax.slice_in_dim(field, 1, count, axis=axis)
    return jnp.concatenate([rest, jnp.zeros_like(lax.slice_in_dim(field, 0, 1, axis=axis))], axis)


def behind(field, axis):
    count = field.shape[axis]
    rest = lax.slice_in_dim(field, 0, count - 1, axis=axis)
    return jnp.concatenate([jnp.zeros_like(lax.slice_in_dim(field, 0, 1, axis=axis)), rest], axis)


def coupling(field, shear, spring):
    return (
        jnp.stack(
            [
                field[0] + shear[0] * field[1] + shear[1] * field[2],
                shear[0] * field[0] + field[1] + shear[2] * field[2],
                shear[1] * field[0] + shear[2] * field[1] + field[2],
            ]
        )
        * spring
    )


def stepwise(sensitivity, stiffness, spring, shear, live, inter):
    rows_az, rows_span, slots = stiffness.shape
    padded = padded_2(jnp.stack([stiffness, live]), (("azimuth", 1), ("span", 2)), 1)
    kpad = padded[0]
    lpad = padded[1]
    w_ap = live * lpad[2:, 1:-1] * (stiffness + kpad[2:, 1:-1]) * 0.5
    w_am = live * lpad[:-2, 1:-1] * (stiffness + kpad[:-2, 1:-1]) * 0.5
    w_sp = live * lpad[1:-1, 2:] * (stiffness + kpad[1:-1, 2:]) * 0.5
    w_sm = live * lpad[1:-1, :-2] * (stiffness + kpad[1:-1, :-2]) * 0.5
    span_rank = lax.axis_index("span")
    span_count = lax.axis_size("span")
    row = lax.broadcasted_iota(jnp.int32, stiffness.shape, 1)
    top_edge = jnp.logical_and(span_rank == span_count - 1, row == rows_span - 1)
    low_edge = jnp.logical_and(span_rank == 0, row == 0)
    w_sp = jnp.where(top_edge, 0.0, w_sp)
    w_sm = jnp.where(low_edge, 0.0, w_sm)
    w_zp = live * ahead(live, 2) * (stiffness + ahead(stiffness, 2)) * 0.5
    w_zm = live * behind(live, 2) * (stiffness + behind(stiffness, 2)) * 0.5
    residual = live * sensitivity
    solution_field = jnp.zeros_like(residual)

    def squares(vector):
        return lax.psum(jnp.sum(vector * vector), ("azimuth", "span"))

    def iteration(step, carry):
        solution_field, residual, direction, norm_now = carry
        extended = padded_2(direction, (("azimuth", 1), ("span", 2)), 1)
        next_az = extended[:, 2:, 1:-1]
        prev_az = extended[:, :-2, 1:-1]
        next_span = extended[:, 1:-1, 2:]
        prev_span = extended[:, 1:-1, :-2]
        lap = w_ap * (direction - next_az) + w_am * (direction - prev_az)
        lap = lap + w_sp * (direction - next_span) + w_sm * (direction - prev_span)
        lap = (
            lap
            + w_zp * (direction - ahead(direction, 3))
            + w_zm * (direction - behind(direction, 3))
        )
        coupled = coupling(direction, shear, spring)
        image = live * (lap + coupled + penalty_weight * inter * direction)
        alpha = norm_now / lax.psum(jnp.sum(direction * image), ("azimuth", "span"))
        solution_field = solution_field + alpha * direction
        residual = residual - alpha * image
        norm_next = squares(residual)
        direction = residual + norm_next / norm_now * direction
        return solution_field, residual, direction, norm_next

    carry = (solution_field, residual, residual, squares(residual))
    carry = lax.fori_loop(0, ITERS, iteration, carry)
    return carry[0], carry[1]


FIELDS = 8
TILE = 8


def call(kernel, shapes, n_in, smem=(), scratch=()):
    return pl.pallas_call(
        kernel,
        out_shape=[jax.ShapeDtypeStruct(s, F32) for s in shapes],
        in_specs=[SMEM if i in smem else VMEM for i in range(n_in)],
        out_specs=[VMEM] * len(shapes),
        scratch_shapes=[pltpu.VMEM(s, F32) for s in scratch],
        compiler_params=pltpu.CompilerParams(vmem_limit_bytes=32 << 20),
    )


def reach(f):
    return 2 if f < 4 else 1


def place(f, d):
    return 2 * f + d - 1 if f < 4 else 4 + f


STRIP = 12
CORNER = 6
RELAY = CORNER + 5


def even(axis):
    return lax.axis_index(axis) % 2 == 0


def sublane(slots):
    return lax.broadcasted_iota(jnp.int32, (TILE, slots), 0)


def turn(x, shift, axis):
    shift = shift % x.shape[axis]
    return pltpu.roll(x, shift, axis) if shift else x


def packed_rows(tiles, sign):
    s = sublane(tiles[0].shape[1])
    s = s if sign > 0 else TILE - 1 - s
    out = [jnp.where(s < 3, tiles[f], turn(tiles[f + 1], sign * 3, 0)) for f in (0, 2)]
    last = tiles[4]
    for j in range(1, 4):
        last = jnp.where(s < 2 * j, last, turn(tiles[4 + j], sign * 2 * j, 0))
    return out + [last]


def unpacked(ref, f, a, sign):
    tile = ref[3 * a + (f // 2 if f < 4 else 2)]
    return turn(tile, -sign * (3 * (f % 2) if f < 4 else 2 * (f - 4)), 0)


def pack_kernel(blocks_ref, s_ref, k_ref, spring_ref, shear_ref, inter_ref, own_ref, me_ref, mo_ref, se_ref, so_ref):
    n_az, n_sp, slots = k_ref.shape
    blocks = inter_ref.shape[1]
    width = slots // blocks
    zpos = lax.broadcasted_iota(jnp.int32, (n_sp, slots), 1)
    live = zpos < jnp.broadcast_to(blocks_ref[...] * width, (n_sp, slots))
    same = lax.broadcasted_iota(jnp.int32, (n_sp, n_sp), 0) == lax.broadcasted_iota(jnp.int32, (n_sp, n_sp), 1)
    for a in range(n_az):
        spring = spring_ref[a]
        flags = inter_ref[a].astype(F32)
        columns = []
        for b in range(blocks):
            row = jnp.broadcast_to(flags[b : b + 1, :], (n_sp, n_sp))
            column = jnp.sum(jnp.where(same, row, 0.0), axis=1, keepdims=True)
            columns.append(jnp.broadcast_to(column, (n_sp, width)))
        inter = jnp.concatenate(columns, axis=1)
        fields = [s_ref[c, a] for c in range(3)] + [k_ref[a], spring + penalty_weight * inter]
        fields += [shear_ref[i, a] * spring for i in range(3)]
        fields = [jnp.where(live, v, 0.0) for v in fields]
        for f, v in enumerate(fields):
            own_ref[f, a] = v
        first = packed_rows([v[:TILE] for v in fields], 1)
        last = packed_rows([v[n_sp - TILE :] for v in fields], -1)
        up = even("span")
        for n in range(3):
            se_ref[3 * a + n] = jnp.where(up, last[n], first[n])
            so_ref[3 * a + n] = jnp.where(up, first[n], last[n])
    flip = even("azimuth")
    for f in range(FIELDS):
        for d in range(1, reach(f) + 1):
            me_ref[place(f, d)] = own_ref[f, jnp.where(flip, n_az - d, d - 1)]
            mo_ref[place(f, d)] = own_ref[f, jnp.where(flip, d - 1, n_az - d)]


def face(k, near):
    return jnp.where(jnp.minimum(k, near) > 0.0, (k + near) * 0.5, 0.0)


def layer_weights(k, lane):
    slots = k.shape[1]
    return face(k, turn(k, -1, 0)), face(k, jnp.where(lane == slots - 1, 0.0, turn(k, -1, 1)))


def local_diagonal(k, ws, wz, fixed):
    return (ws + turn(ws, 1, 0)) + (wz + turn(wz, 1, 1)) + (fixed - jnp.where(k > 0.0, SHIFT, 0.0))


def image_of(get, off, wl, wh, ws, wz, diag, a):
    u = [get(c, a) for c in range(3)]
    mixed = [off[0] * u[1] + off[1] * u[2], off[0] * u[0] + off[2] * u[2], off[1] * u[0] + off[2] * u[1]]
    out = []
    for c in range(3):
        acc = wh * get(c, a + 1) + wl * get(c, a - 1)
        acc = acc + (ws * turn(u[c], -1, 0) + turn(ws * u[c], 1, 0))
        acc = acc + (wz * turn(u[c], -1, 1) + turn(wz * u[c], 1, 1))
        out.append(diag * u[c] + mixed[c] - acc)
    return out


def side_kernel(own, se_ref, so_ref, near_ref, re_ref, ro_ref, u1_ref, wa_ref, ws_ref, wz_ref, diag_ref):
    n_az, n_sp, slots = own.shape[1:]
    s = lax.broadcasted_iota(jnp.int32, (TILE, slots), 0)
    lane = lax.broadcasted_iota(jnp.int32, (n_sp + TILE, slots), 1)
    up, flip = even("span"), even("azimuth")
    for a in range(n_az):
        after = {3 * a + n: jnp.where(up, se_ref[3 * a + n], so_ref[3 * a + n]) for n in range(3)}
        before = {3 * a + n: jnp.where(up, so_ref[3 * a + n], se_ref[3 * a + n]) for n in range(3)}
        for f in range(FIELDS):
            near_ref[f * n_az + a] = jnp.where(
                s < TILE // 2, unpacked(after, f, a, 1), unpacked(before, f, a, -1)
            )

    def field(f, a):
        return jnp.concatenate([own[f, a], near_ref[f * n_az + a]], axis=0)

    for a in range(n_az):
        k = field(3, a)
        ws, wz = layer_weights(k, lane)
        ws_ref[a], wz_ref[a] = ws, wz
        diag = local_diagonal(k, ws, wz, field(4, a))
        if a + 1 < n_az:
            wa_ref[a] = face(k, field(3, a + 1))
            diag = diag + wa_ref[a]
        diag_ref[a] = diag + wa_ref[a - 1] if a > 0 else diag
    for a in range(1, n_az - 1):
        off = [field(5 + i, a) for i in range(3)]
        image = image_of(field, off, wa_ref[a - 1], wa_ref[a], ws_ref[a], wz_ref[a], diag_ref[a], a)
        for c, v in enumerate(image):
            u1_ref[c, a - 1] = v

    def corner(one, step):
        out = []
        for c in range(3):
            v = u1_ref[c, one + step - 1]
            out += [v[:TILE], v[TILE:n_sp]]
        for f in range(4):
            near, far = near_ref[f * n_az + one], near_ref[f * n_az + one + step]
            out.append(jnp.where(s == 2, turn(far, 2, 0), jnp.where(s == TILE - 3, turn(far, -2, 0), near)))
        packed = near_ref[4 * n_az + one]
        for j in range(1, 4):
            v = near_ref[(4 + j) * n_az + one]
            packed = jnp.where(s == j, turn(v, j, 0), jnp.where(s == TILE - 1 - j, turn(v, -j, 0), packed))
        return out + [packed]

    for n, (low, high) in enumerate(zip(corner(0, 1), corner(n_az - 1, -1))):
        re_ref[n] = jnp.where(flip, high, low)
        ro_ref[n] = jnp.where(flip, low, high)


PAIRS = ((0, 0), (0, 1), (0, 2), (0, 3), (1, 1), (1, 2), (1, 3), (2, 2), (2, 3), (3, 3))


def folded(x):
    n, m = x.shape
    x = x.reshape(n // 8, 8, m).sum(0) if n > 8 else x
    out = x[:, 0:128]
    for b in range(1, m // 128):
        out = out + x[:, b * 128 : (b + 1) * 128]
    return out


def basis_kernel(own, near, me, mo, re, ro, *rest):
    flip = even("azimuth")

    @pl.when(flip)
    def _():
        basis(own, near, (mo, ro), (me, re), *rest)

    @pl.when(jnp.logical_not(flip))
    def _():
        basis(own, near, (me, re), (mo, ro), *rest)


def basis(own, near, low, high, mid, wa, ws, wz, diag, u1_ref, u2_ref, u3_ref, sums_ref, wa_out, ws_out, wz_out, diag_out):
    n_az, n_sp, slots = own.shape[1:]
    s = lax.broadcasted_iota(jnp.int32, (TILE, slots), 0)
    lane = lax.broadcasted_iota(jnp.int32, (n_sp + TILE, slots), 1)
    ends = (-1, n_az)

    def field(f, a):
        if 0 <= a < n_az:
            return jnp.concatenate([own[f, a], near[f * n_az + a]], axis=0)
        (side, relay), d = (high, a - n_az + 1) if a >= n_az else (low, -a)
        if f < 4:
            tile = relay[CORNER + f]
            if d == 2:
                tile = jnp.where(s < TILE // 2, turn(tile, -2, 0), turn(tile, 2, 0))
        else:
            j = f - 4
            tile = relay[CORNER + 4]
            tile = jnp.where(s < TILE // 2, turn(tile, -j, 0), turn(tile, j, 0))
        return jnp.concatenate([side[place(f, d)], tile], axis=0)

    outer = {-2: 0, -1: 1, n_az - 1: 2, n_az: 3}
    for a, n in outer.items():
        wa_out[n] = face(field(3, a), field(3, a + 1))
    for n, a in enumerate(ends):
        k = field(3, a)
        ws_out[n], wz_out[n] = layer_weights(k, lane)
        total = local_diagonal(k, ws_out[n], wz_out[n], field(4, a))
        diag_out[n] = total + wa_out[outer[a - 1]] + wa_out[outer[a]]
    diag_out[2] = diag[0] + wa_out[outer[-1]]
    diag_out[3] = diag[n_az - 1] + wa_out[outer[n_az - 1]]

    def between(a):
        return wa_out[outer[a]] if a in outer else wa[a]

    def image(get, a):
        n = ends.index(a) if a in ends else None
        rows, slot = (ws_out[n], wz_out[n]) if a in ends else (ws[a], wz[a])
        middle = diag_out[n] if a in ends else diag_out[2] if a == 0 else diag_out[3] if a == n_az - 1 else diag[a]
        off = [field(5 + i, a) for i in range(3)]
        return image_of(get, off, between(a - 1), between(a), rows, slot, middle, a)

    def first(c, a):
        if 0 < a < n_az - 1:
            return mid[c, a - 1]
        if -1 <= a <= n_az:
            return u1_ref[c, a + 1]
        relay = high[1] if a > 0 else low[1]
        return jnp.concatenate([relay[2 * c], relay[2 * c + 1], jnp.zeros((TILE, slots), F32)], axis=0)

    for a in (-1, 0, n_az - 1, n_az):
        for c, v in enumerate(image(field, a)):
            u1_ref[c, a + 1] = v
    for a in range(-1, n_az + 1):
        for c, v in enumerate(image(first, a)):
            u2_ref[c, a + 1] = v
    acc = [jnp.zeros((8, 128), F32) for _ in PAIRS]
    for a in range(n_az):
        for c, v in enumerate(image(lambda c, b: u2_ref[c, b + 1], a)):
            v = v[:n_sp]
            u3_ref[c, a] = v
            u = [own[c, a], first(c, a)[:n_sp], u2_ref[c, a + 1][:n_sp], v]
            for n, (i, j) in enumerate(PAIRS):
                acc[n] = acc[n] + folded(u[i] * u[j])
    lane = lax.broadcasted_iota(jnp.int32, (8, 128), 1)
    total = jnp.zeros((8, 128), F32)
    for n in range(len(PAIRS)):
        one = jnp.sum(jnp.sum(acc[n], axis=0, keepdims=True), axis=1, keepdims=True)
        total = jnp.where(lane == n, one, total)
    sums_ref[...] = total


def coefficients(rows):
    lane = lax.broadcasted_iota(jnp.int32, (8, 128), 1)
    row = jnp.broadcast_to(jnp.sum(rows, axis=0, keepdims=True), (8, 128))

    def entry(n):
        return jnp.broadcast_to(jnp.sum(jnp.where(lane == n, row, 0.0), axis=1, keepdims=True), (8, 128))

    g = {p: entry(n) for n, p in enumerate(PAIRS)}
    n0 = g[0, 0]
    m10, m20, m30 = g[0, 1] / n0, g[0, 2] / n0, g[0, 3] / n0
    n1 = g[1, 1] - m10 * g[0, 1]
    t21 = g[1, 2] - m10 * g[0, 2]
    t31 = g[1, 3] - m10 * g[0, 3]
    m21, m31 = t21 / n1, t31 / n1
    n2 = g[2, 2] - m20 * g[0, 2] - m21 * t21
    t32 = g[2, 3] - m20 * g[0, 3] - m21 * t31
    m32 = t32 / n2
    n3 = g[3, 3] - m30 * g[0, 3] - m31 * t31 - m32 * t32
    b0, b1, b2 = SHIFT + m10, SHIFT + m21 - m10, SHIFT + m32 - m21
    g1, g2 = n1 / n0, n2 / n1
    a0 = 1.0 / b0
    a1 = 1.0 / (b1 - g1 * a0)
    a2 = 1.0 / (b2 - g2 * a1)
    safe = jnp.logical_and(
        jnp.logical_and(n1 > SAFE * g[1, 1], n2 > SAFE * g[2, 2]),
        jnp.logical_and(n3 > SAFE * g[3, 3], jnp.logical_and(a1 > 0.0, a2 > 0.0)),
    )
    f = {"m10": m10, "m20": m20, "m21": m21, "m30": m30, "m31": m31, "m32": m32}
    f["e1"], f["e2"] = a0 * g1, a1 * g2
    f["x0"], f["x1"], f["x2"] = a0, -(a0 * a1), a0 * a1 * a2
    f["r3"] = -(a0 * a1 * a2)
    return f, safe


def final_kernel(rows_ref, u0_ref, mid_ref, u1_ref, u2_ref, u3_ref, x_ref, r_ref, safe_ref):
    f, safe = coefficients(rows_ref[...])
    safe_ref[...] = jnp.where(safe, 1.0, 0.0)[0:1, 0:1]
    n_az, n_sp, slots = u3_ref.shape[1:]
    f = {key: jnp.concatenate([jnp.concatenate([v] * (n_sp // 8), 0)] * (slots // 128), 1) for key, v in f.items()}
    for c in range(3):
        for a in range(n_az):
            u1 = mid_ref[c, a - 1] if 0 < a < n_az - 1 else u1_ref[c, a + 1]
            u0, u1, u2, u3 = u0_ref[c, a], u1[:n_sp], u2_ref[c, a + 1][:n_sp], u3_ref[c, a]
            q1 = u1 - f["m10"] * u0
            q2 = u2 - f["m21"] * q1 - f["m20"] * u0
            q3 = u3 - f["m32"] * q2 - f["m31"] * q1 - f["m30"] * u0
            p1 = q1 - f["e1"] * u0
            p2 = q2 - f["e2"] * p1
            x_ref[c, a] = f["x0"] * u0 + f["x1"] * p1 + f["x2"] * p2
            r_ref[c, a] = f["r3"] * q3


def swaps(evens, odds, axis, wraps):
    n = lax.axis_size(axis)
    first = [(i, i + 1) for i in range(0, n, 2)]
    second = [(i, (i + 1) % n) for i in range(1, n if wraps else n - 1, 2)]
    return [
        lax.ppermute(v, axis, pairs + [(j, i) for i, j in pairs]) for v, pairs in ((evens, first), (odds, second))
    ]


def everywhere(row, axis):
    n = lax.axis_size(axis)
    return lax.all_to_all(jnp.broadcast_to(row, (n, 128)), axis, 0, 0, tiled=True)


def on_device(sensitivity, stiffness, spring, shear, interface, live_blocks):
    rows_az, rows_span, slots = stiffness.shape
    blocks = interface.shape[2]
    width = slots // blocks
    field = (3, rows_az, rows_span, slots)
    strip = (STRIP, rows_span, slots)
    tiles = (3 * rows_az, TILE, slots)
    own, me, mo, se, so = call(pack_kernel, [(FIELDS,) + field[1:], strip, strip, tiles, tiles], 6)(
        live_blocks, sensitivity, stiffness, spring, shear, jnp.transpose(interface, (0, 2, 1))
    )
    se, so = swaps(se, so, "span", False)
    me, mo = swaps(me, mo, "azimuth", True)
    tall = (rows_span + TILE, slots)
    relay = (RELAY, TILE, slots)
    inner = [(rows_az - 1,) + tall] + [(rows_az,) + tall] * 3
    near, re, ro, mid, *weights = call(
        side_kernel, [(FIELDS * rows_az, TILE, slots), relay, relay, (3, rows_az - 2) + tall] + inner, 3
    )(own, se, so)
    re, ro = swaps(re, ro, "azimuth", True)
    u1, u2, u3, sums = call(
        basis_kernel,
        [(3, rows_az + 2) + tall, (3, rows_az + 2) + tall, field, (8, 128)],
        11,
        scratch=((4,) + tall, (2,) + tall, (2,) + tall, (4,) + tall),
    )(own, near, me, mo, re, ro, mid, *weights)
    sums = jnp.sum(everywhere(sums[0:1], "span"), axis=0, keepdims=True)
    rows = everywhere(sums, "azimuth")
    rows, sensitivity, stiffness, spring, shear, interface, live_blocks = lax.optimization_barrier(
        (rows, sensitivity, stiffness, spring, shear, interface, live_blocks)
    )
    x, res, safe = call(final_kernel, [field, field, (1, 1)], 6)(rows, own, mid, u1, u2, u3)

    def guarded():
        zpos = lax.broadcasted_iota(jnp.int32, stiffness.shape, 2)
        live = (zpos < live_blocks[0, 0] * width).astype(F32)
        inter = jnp.broadcast_to(interface[:, :, :, None], (rows_az, rows_span, blocks, width))
        inter = inter.reshape(stiffness.shape).astype(F32)
        return stepwise(sensitivity, stiffness, spring, shear, live, inter)

    return lax.cond(safe[0, 0] > 0.5, lambda: (x, res), guarded)


def solution(mesh):
    return jax.shard_map(
        on_device,
        mesh=mesh,
        in_specs=(
            P(None, "azimuth", "span", None),
            P("azimuth", "span", None),
            P("azimuth", "span", None),
            P(None, "azimuth", "span", None),
            P("azimuth", "span", None),
            P("azimuth", "span"),
        ),
        out_specs=(P(None, "azimuth", "span", None), P(None, "azimuth", "span", None)),
        check_vma=False,
    )
```

```python
import jax
import jax.numpy as jnp
from jax import lax
from jax.experimental import pallas as pl
from jax.experimental.pallas import tpu as pltpu
from jax.sharding import PartitionSpec as P


ITERS = 3
penalty_weight = 4.0
SHIFT = 5.0
SAFE = 0.01
F32 = jnp.float32
VMEM = pl.BlockSpec(memory_space=pltpu.VMEM)


def padded_2(x, sides, width):
    for axis, dim in sides:
        peers, length = (lax.axis_size(axis), x.shape[dim])
        up = [(i, (i + 1) % peers) for i in range(peers)]
        down = [(j, i) for i, j in up]
        last = lax.slice_in_dim(x, length - width, length, axis=dim)
        leading = lax.slice_in_dim(x, 0, width, axis=dim)
        before = lax.ppermute(last, axis, up)
        after = lax.ppermute(leading, axis, down)
        x = jnp.concatenate([before, x, after], axis=dim)
    return x


def ahead(field, axis):
    count = field.shape[axis]
    rest = lax.slice_in_dim(field, 1, count, axis=axis)
    return jnp.concatenate([rest, jnp.zeros_like(lax.slice_in_dim(field, 0, 1, axis=axis))], axis)


def behind(field, axis):
    count = field.shape[axis]
    rest = lax.slice_in_dim(field, 0, count - 1, axis=axis)
    return jnp.concatenate([jnp.zeros_like(lax.slice_in_dim(field, 0, 1, axis=axis)), rest], axis)


def coupling(field, shear, spring):
    return (
        jnp.stack(
            [
                field[0] + shear[0] * field[1] + shear[1] * field[2],
                shear[0] * field[0] + field[1] + shear[2] * field[2],
                shear[1] * field[0] + shear[2] * field[1] + field[2],
            ]
        )
        * spring
    )


def stepwise(sensitivity, stiffness, spring, shear, live, inter):
    _, rows_span, _ = stiffness.shape
    padded = padded_2(jnp.stack([stiffness, live]), (("azimuth", 1), ("span", 2)), 1)
    kpad = padded[0]
    lpad = padded[1]
    w_ap = live * lpad[2:, 1:-1] * (stiffness + kpad[2:, 1:-1]) * 0.5
    w_am = live * lpad[:-2, 1:-1] * (stiffness + kpad[:-2, 1:-1]) * 0.5
    w_sp = live * lpad[1:-1, 2:] * (stiffness + kpad[1:-1, 2:]) * 0.5
    w_sm = live * lpad[1:-1, :-2] * (stiffness + kpad[1:-1, :-2]) * 0.5
    span_rank = lax.axis_index("span")
    span_count = lax.axis_size("span")
    row = lax.broadcasted_iota(jnp.int32, stiffness.shape, 1)
    top_edge = jnp.logical_and(span_rank == span_count - 1, row == rows_span - 1)
    low_edge = jnp.logical_and(span_rank == 0, row == 0)
    w_sp = jnp.where(top_edge, 0.0, w_sp)
    w_sm = jnp.where(low_edge, 0.0, w_sm)
    w_zp = live * ahead(live, 2) * (stiffness + ahead(stiffness, 2)) * 0.5
    w_zm = live * behind(live, 2) * (stiffness + behind(stiffness, 2)) * 0.5
    residual = live * sensitivity
    solution_field = jnp.zeros_like(residual)

    def squares(vector):
        return lax.psum(jnp.sum(vector * vector), ("azimuth", "span"))

    def iteration(step, carry):
        solution_field, residual, direction, norm_now = carry
        extended = padded_2(direction, (("azimuth", 1), ("span", 2)), 1)
        next_az = extended[:, 2:, 1:-1]
        prev_az = extended[:, :-2, 1:-1]
        next_span = extended[:, 1:-1, 2:]
        prev_span = extended[:, 1:-1, :-2]
        lap = w_ap * (direction - next_az) + w_am * (direction - prev_az)
        lap = lap + w_sp * (direction - next_span) + w_sm * (direction - prev_span)
        lap = (
            lap
            + w_zp * (direction - ahead(direction, 3))
            + w_zm * (direction - behind(direction, 3))
        )
        coupled = coupling(direction, shear, spring)
        image = live * (lap + coupled + penalty_weight * inter * direction)
        alpha = norm_now / lax.psum(jnp.sum(direction * image), ("azimuth", "span"))
        solution_field = solution_field + alpha * direction
        residual = residual - alpha * image
        norm_next = squares(residual)
        direction = residual + norm_next / norm_now * direction
        return solution_field, residual, direction, norm_next

    carry = (solution_field, residual, residual, squares(residual))
    carry = lax.fori_loop(0, ITERS, iteration, carry)
    return carry[0], carry[1]


FIELDS = 8
TILE = 8


def call(kernel, shapes, n_in, scratch=()):
    return pl.pallas_call(
        kernel,
        out_shape=[jax.ShapeDtypeStruct(s, F32) for s in shapes],
        in_specs=[VMEM] * n_in,
        out_specs=[VMEM] * len(shapes),
        scratch_shapes=[pltpu.VMEM(s, F32) for s in scratch],
        compiler_params=pltpu.CompilerParams(vmem_limit_bytes=32 << 20),
    )


def reach(f):
    return 2 if f < 4 else 1


def place(f, d):
    return 2 * f + d - 1 if f < 4 else 4 + f


STRIP = 12
CORNER = 6
RELAY = CORNER + 5


def even(axis):
    return lax.axis_index(axis) % 2 == 0


def sublane(slots):
    return lax.broadcasted_iota(jnp.int32, (TILE, slots), 0)


def turn(x, shift, axis):
    shift = shift % x.shape[axis]
    return pltpu.roll(x, shift, axis) if shift else x


def packed_rows(tiles, sign):
    s = sublane(tiles[0].shape[1])
    s = s if sign > 0 else TILE - 1 - s
    out = [jnp.where(s < 3, tiles[f], turn(tiles[f + 1], sign * 3, 0)) for f in (0, 2)]
    last = tiles[4]
    for j in range(1, 4):
        last = jnp.where(s < 2 * j, last, turn(tiles[4 + j], sign * 2 * j, 0))
    return out + [last]


def unpacked(ref, f, a, sign):
    tile = ref[3 * a + (f // 2 if f < 4 else 2)]
    return turn(tile, -sign * (3 * (f % 2) if f < 4 else 2 * (f - 4)), 0)


def pack_kernel(*refs):
    count, stored, outs, copied, sems = refs[0], refs[1:6], refs[6:11], refs[11:16], refs[16]
    own_ref, me_ref, mo_ref, se_ref, so_ref = outs
    s_ref, k_ref, spring_ref, shear_ref, inter_ref = copied
    n_az, n_sp, slots = k_ref.shape
    blocks = inter_ref.shape[1]
    width = slots // blocks

    def fetches(a):
        out = []
        for n, (src, dst) in enumerate(zip(stored, copied)):
            at = (slice(None), a) if len(src.shape) == 4 else (a,)
            out.append(pltpu.make_async_copy(src.at[at], dst.at[at], sems.at[a, n]))
        return out

    for a in range(n_az):
        for fetch in fetches(a):
            fetch.start()
    zpos = lax.broadcasted_iota(jnp.int32, (n_sp, slots), 1)
    live = zpos < count[0, 0] * width
    same = lax.broadcasted_iota(jnp.int32, (n_sp, n_sp), 0) == lax.broadcasted_iota(jnp.int32, (n_sp, n_sp), 1)
    for a in range(n_az):
        for fetch in fetches(a):
            fetch.wait()
        spring = spring_ref[a]
        flags = inter_ref[a].astype(F32)
        columns = []
        for b in range(blocks):
            row = jnp.broadcast_to(flags[b : b + 1, :], (n_sp, n_sp))
            column = jnp.sum(jnp.where(same, row, 0.0), axis=1, keepdims=True)
            columns.append(jnp.broadcast_to(column, (n_sp, width)))
        inter = jnp.concatenate(columns, axis=1)
        fields = [s_ref[c, a] for c in range(3)] + [k_ref[a], spring + penalty_weight * inter]
        fields += [shear_ref[i, a] * spring for i in range(3)]
        fields = [jnp.where(live, v, 0.0) for v in fields]
        for f, v in enumerate(fields):
            own_ref[f, a] = v
        first = packed_rows([v[:TILE] for v in fields], 1)
        last = packed_rows([v[n_sp - TILE :] for v in fields], -1)
        up = even("span")
        for n in range(3):
            se_ref[3 * a + n] = jnp.where(up, last[n], first[n])
            so_ref[3 * a + n] = jnp.where(up, first[n], last[n])
    flip = even("azimuth")
    for f in range(FIELDS):
        for d in range(1, reach(f) + 1):
            me_ref[place(f, d)] = own_ref[f, jnp.where(flip, n_az - d, d - 1)]
            mo_ref[place(f, d)] = own_ref[f, jnp.where(flip, d - 1, n_az - d)]


def face(k, near):
    return jnp.where(jnp.minimum(k, near) > 0.0, (k + near) * 0.5, 0.0)


def layer_weights(k, lane):
    slots = k.shape[1]
    return face(k, turn(k, -1, 0)), face(k, jnp.where(lane == slots - 1, 0.0, turn(k, -1, 1)))


def local_diagonal(k, ws, wz, fixed):
    return (ws + turn(ws, 1, 0)) + (wz + turn(wz, 1, 1)) + (fixed - jnp.where(k > 0.0, SHIFT, 0.0))


def image_of(get, off, wl, wh, ws, wz, diag, a):
    u = [get(c, a) for c in range(3)]
    mixed = [off[0] * u[1] + off[1] * u[2], off[0] * u[0] + off[2] * u[2], off[1] * u[0] + off[2] * u[1]]
    out = []
    for c in range(3):
        acc = wh * get(c, a + 1) + wl * get(c, a - 1)
        acc = acc + (ws * turn(u[c], -1, 0) + turn(ws * u[c], 1, 0))
        acc = acc + (wz * turn(u[c], -1, 1) + turn(wz * u[c], 1, 1))
        out.append(diag * u[c] + mixed[c] - acc)
    return out


def side_kernel(own, se_ref, so_ref, near_ref, re_ref, ro_ref, u1_ref, wa_ref, ws_ref, wz_ref, diag_ref):
    n_az, n_sp, slots = own.shape[1:]
    s = lax.broadcasted_iota(jnp.int32, (TILE, slots), 0)
    lane = lax.broadcasted_iota(jnp.int32, (n_sp + TILE, slots), 1)
    up, flip = even("span"), even("azimuth")
    for a in range(n_az):
        after = {3 * a + n: jnp.where(up, se_ref[3 * a + n], so_ref[3 * a + n]) for n in range(3)}
        before = {3 * a + n: jnp.where(up, so_ref[3 * a + n], se_ref[3 * a + n]) for n in range(3)}
        for f in range(FIELDS):
            near_ref[f * n_az + a] = jnp.where(
                s < TILE // 2, unpacked(after, f, a, 1), unpacked(before, f, a, -1)
            )

    def field(f, a):
        return jnp.concatenate([own[f, a], near_ref[f * n_az + a]], axis=0)

    for a in range(n_az):
        k = field(3, a)
        ws, wz = layer_weights(k, lane)
        ws_ref[a], wz_ref[a] = ws, wz
        diag = local_diagonal(k, ws, wz, field(4, a))
        if a + 1 < n_az:
            wa_ref[a] = face(k, field(3, a + 1))
            diag = diag + wa_ref[a]
        diag_ref[a] = diag + wa_ref[a - 1] if a > 0 else diag
    for a in range(1, n_az - 1):
        off = [field(5 + i, a) for i in range(3)]
        image = image_of(field, off, wa_ref[a - 1], wa_ref[a], ws_ref[a], wz_ref[a], diag_ref[a], a)
        for c, v in enumerate(image):
            u1_ref[c, a - 1] = v

    def corner(one, step):
        out = []
        for c in range(3):
            v = u1_ref[c, one + step - 1]
            out += [v[:TILE], v[TILE:n_sp]]
        for f in range(4):
            near, far = near_ref[f * n_az + one], near_ref[f * n_az + one + step]
            out.append(jnp.where(s == 2, turn(far, 2, 0), jnp.where(s == TILE - 3, turn(far, -2, 0), near)))
        packed = near_ref[4 * n_az + one]
        for j in range(1, 4):
            v = near_ref[(4 + j) * n_az + one]
            packed = jnp.where(s == j, turn(v, j, 0), jnp.where(s == TILE - 1 - j, turn(v, -j, 0), packed))
        return out + [packed]

    for n, (low, high) in enumerate(zip(corner(0, 1), corner(n_az - 1, -1))):
        re_ref[n] = jnp.where(flip, high, low)
        ro_ref[n] = jnp.where(flip, low, high)


PAIRS = ((0, 0), (0, 1), (0, 2), (0, 3), (1, 1), (1, 2), (1, 3), (2, 2), (2, 3), (3, 3))


def folded(x):
    n, m = x.shape
    x = x.reshape(n // 8, 8, m).sum(0) if n > 8 else x
    out = x[:, 0:128]
    for b in range(1, m // 128):
        out = out + x[:, b * 128 : (b + 1) * 128]
    return out


def basis_kernel(own, near, me, mo, re, ro, *rest):
    flip = even("azimuth")

    @pl.when(flip)
    def _():
        basis(own, near, (mo, ro), (me, re), *rest)

    @pl.when(jnp.logical_not(flip))
    def _():
        basis(own, near, (me, re), (mo, ro), *rest)


def basis(own, near, low, high, mid, wa, ws, wz, diag, u1_ref, u2_ref, u3_ref, sums_ref, wa_out, ws_out, wz_out, diag_out):
    n_az, n_sp, slots = own.shape[1:]
    s = lax.broadcasted_iota(jnp.int32, (TILE, slots), 0)
    lane = lax.broadcasted_iota(jnp.int32, (n_sp + TILE, slots), 1)
    ends = (-1, n_az)

    def field(f, a):
        if 0 <= a < n_az:
            return jnp.concatenate([own[f, a], near[f * n_az + a]], axis=0)
        (side, relay), d = (high, a - n_az + 1) if a >= n_az else (low, -a)
        if f < 4:
            tile = relay[CORNER + f]
            if d == 2:
                tile = jnp.where(s < TILE // 2, turn(tile, -2, 0), turn(tile, 2, 0))
        else:
            j = f - 4
            tile = relay[CORNER + 4]
            tile = jnp.where(s < TILE // 2, turn(tile, -j, 0), turn(tile, j, 0))
        return jnp.concatenate([side[place(f, d)], tile], axis=0)

    outer = {-2: 0, -1: 1, n_az - 1: 2, n_az: 3}
    for a, n in outer.items():
        wa_out[n] = face(field(3, a), field(3, a + 1))
    for n, a in enumerate(ends):
        k = field(3, a)
        ws_out[n], wz_out[n] = layer_weights(k, lane)
        total = local_diagonal(k, ws_out[n], wz_out[n], field(4, a))
        diag_out[n] = total + wa_out[outer[a - 1]] + wa_out[outer[a]]
    diag_out[2] = diag[0] + wa_out[outer[-1]]
    diag_out[3] = diag[n_az - 1] + wa_out[outer[n_az - 1]]

    def between(a):
        return wa_out[outer[a]] if a in outer else wa[a]

    def image(get, a):
        n = ends.index(a) if a in ends else None
        rows, slot = (ws_out[n], wz_out[n]) if a in ends else (ws[a], wz[a])
        middle = diag_out[n] if a in ends else diag_out[2] if a == 0 else diag_out[3] if a == n_az - 1 else diag[a]
        off = [field(5 + i, a) for i in range(3)]
        return image_of(get, off, between(a - 1), between(a), rows, slot, middle, a)

    def first(c, a):
        if 0 < a < n_az - 1:
            return mid[c, a - 1]
        if -1 <= a <= n_az:
            return u1_ref[c, a + 1]
        relay = high[1] if a > 0 else low[1]
        return jnp.concatenate([relay[2 * c], relay[2 * c + 1], jnp.zeros((TILE, slots), F32)], axis=0)

    for a in (-1, 0, n_az - 1, n_az):
        for c, v in enumerate(image(field, a)):
            u1_ref[c, a + 1] = v
    for a in range(-1, n_az + 1):
        for c, v in enumerate(image(first, a)):
            u2_ref[c, a + 1] = v
    acc = [jnp.zeros((8, 128), F32) for _ in PAIRS]
    for a in range(n_az):
        for c, v in enumerate(image(lambda c, b: u2_ref[c, b + 1], a)):
            v = v[:n_sp]
            u3_ref[c, a] = v
            u = [own[c, a], first(c, a)[:n_sp], u2_ref[c, a + 1][:n_sp], v]
            for n, (i, j) in enumerate(PAIRS):
                acc[n] = acc[n] + folded(u[i] * u[j])
    lane = lax.broadcasted_iota(jnp.int32, (8, 128), 1)
    total = jnp.zeros((8, 128), F32)
    for n in range(len(PAIRS)):
        one = jnp.sum(jnp.sum(acc[n], axis=0, keepdims=True), axis=1, keepdims=True)
        total = jnp.where(lane == n, one, total)
    sums_ref[...] = total


def coefficients(rows):
    lane = lax.broadcasted_iota(jnp.int32, (8, 128), 1)
    row = jnp.broadcast_to(jnp.sum(rows, axis=0, keepdims=True), (8, 128))

    def entry(n):
        return jnp.broadcast_to(jnp.sum(jnp.where(lane == n, row, 0.0), axis=1, keepdims=True), (8, 128))

    g = {p: entry(n) for n, p in enumerate(PAIRS)}
    n0 = g[0, 0]
    m10, m20, m30 = g[0, 1] / n0, g[0, 2] / n0, g[0, 3] / n0
    n1 = g[1, 1] - m10 * g[0, 1]
    t21 = g[1, 2] - m10 * g[0, 2]
    t31 = g[1, 3] - m10 * g[0, 3]
    m21, m31 = t21 / n1, t31 / n1
    n2 = g[2, 2] - m20 * g[0, 2] - m21 * t21
    t32 = g[2, 3] - m20 * g[0, 3] - m21 * t31
    m32 = t32 / n2
    n3 = g[3, 3] - m30 * g[0, 3] - m31 * t31 - m32 * t32
    b0, b1, b2 = SHIFT + m10, SHIFT + m21 - m10, SHIFT + m32 - m21
    g1, g2 = n1 / n0, n2 / n1
    a0 = 1.0 / b0
    a1 = 1.0 / (b1 - g1 * a0)
    a2 = 1.0 / (b2 - g2 * a1)
    safe = jnp.logical_and(
        jnp.logical_and(n1 > SAFE * g[1, 1], n2 > SAFE * g[2, 2]),
        jnp.logical_and(n3 > SAFE * g[3, 3], jnp.logical_and(a1 > 0.0, a2 > 0.0)),
    )
    f = {"m10": m10, "m20": m20, "m21": m21, "m30": m30, "m31": m31, "m32": m32}
    f["e1"], f["e2"] = a0 * g1, a1 * g2
    f["x0"], f["x1"], f["x2"] = a0, -(a0 * a1), a0 * a1 * a2
    f["r3"] = -(a0 * a1 * a2)
    return f, safe


def final_kernel(rows_ref, u0_ref, mid_ref, u1_ref, u2_ref, u3_ref, x_ref, r_ref, safe_ref):
    f, safe = coefficients(rows_ref[...])
    safe_ref[...] = jnp.where(safe, 1.0, 0.0)[0:1, 0:1]
    n_az, n_sp, slots = u3_ref.shape[1:]
    f = {key: jnp.concatenate([jnp.concatenate([v] * (n_sp // 8), 0)] * (slots // 128), 1) for key, v in f.items()}
    for c in range(3):
        for a in range(n_az):
            u1 = mid_ref[c, a - 1] if 0 < a < n_az - 1 else u1_ref[c, a + 1]
            u0, u1, u2, u3 = u0_ref[c, a], u1[:n_sp], u2_ref[c, a + 1][:n_sp], u3_ref[c, a]
            q1 = u1 - f["m10"] * u0
            q2 = u2 - f["m21"] * q1 - f["m20"] * u0
            q3 = u3 - f["m32"] * q2 - f["m31"] * q1 - f["m30"] * u0
            p1 = q1 - f["e1"] * u0
            p2 = q2 - f["e2"] * p1
            x_ref[c, a] = f["x0"] * u0 + f["x1"] * p1 + f["x2"] * p2
            r_ref[c, a] = f["r3"] * q3


def swaps(evens, odds, axis, wraps):
    n = lax.axis_size(axis)
    first = [(i, i + 1) for i in range(0, n, 2)]
    second = [(i, (i + 1) % n) for i in range(1, n if wraps else n - 1, 2)]
    out = []
    for v, pairs in ((evens, first), (odds, second)):
        out.append(lax.ppermute(v, axis, pairs + [(j, i) for i, j in pairs]))
    return out


def everywhere(row, axis):
    n = lax.axis_size(axis)
    return lax.all_to_all(jnp.broadcast_to(row, (n, 128)), axis, 0, 0, tiled=True)


def on_device(sensitivity, stiffness, spring, shear, interface, live_blocks):
    rows_az, rows_span, slots = stiffness.shape
    blocks = interface.shape[2]
    width = slots // blocks
    field = (3, rows_az, rows_span, slots)
    strip = (STRIP, rows_span, slots)
    tiles = (3 * rows_az, TILE, slots)
    stored = (sensitivity, stiffness, spring, shear, jnp.transpose(interface, (0, 2, 1)))
    packed = [(FIELDS,) + field[1:], strip, strip, tiles, tiles]
    own, me, mo, se, so = pl.pallas_call(
        pack_kernel,
        out_shape=[jax.ShapeDtypeStruct(v, F32) for v in packed],
        in_specs=[pl.BlockSpec(memory_space=pltpu.SMEM)] + [pl.BlockSpec(memory_space=pltpu.HBM)] * 5,
        out_specs=[VMEM] * 5,
        scratch_shapes=[pltpu.VMEM(v.shape, v.dtype) for v in stored]
        + [pltpu.SemaphoreType.DMA((rows_az, 5))],
        compiler_params=pltpu.CompilerParams(vmem_limit_bytes=32 << 20),
    )(live_blocks, *stored)
    se, so = swaps(se, so, "span", False)
    me, mo = swaps(me, mo, "azimuth", True)
    tall = (rows_span + TILE, slots)
    relay = (RELAY, TILE, slots)
    inner = [(rows_az - 1,) + tall] + [(rows_az,) + tall] * 3
    near, re, ro, mid, *weights = call(
        side_kernel, [(FIELDS * rows_az, TILE, slots), relay, relay, (3, rows_az - 2) + tall] + inner, 3
    )(own, se, so)
    re, ro = swaps(re, ro, "azimuth", True)
    u1, u2, u3, sums = call(
        basis_kernel,
        [(3, rows_az + 2) + tall, (3, rows_az + 2) + tall, field, (8, 128)],
        11,
        scratch=((4,) + tall, (2,) + tall, (2,) + tall, (4,) + tall),
    )(own, near, me, mo, re, ro, mid, *weights)
    sums = jnp.sum(everywhere(sums[0:1], "span"), axis=0, keepdims=True)
    rows = everywhere(sums, "azimuth")
    rows, sensitivity, stiffness, spring, shear, interface = lax.optimization_barrier(
        (rows, sensitivity, stiffness, spring, shear, interface)
    )
    x, res, safe = call(final_kernel, [field, field, (1, 1)], 6)(rows, own, mid, u1, u2, u3)

    def guarded():
        live = (own[3] > 0.0).astype(F32)
        inter = jnp.broadcast_to(interface[:, :, :, None], (rows_az, rows_span, blocks, width))
        inter = inter.reshape(stiffness.shape).astype(F32)
        return stepwise(sensitivity, stiffness, spring, shear, live, inter)

    return lax.cond(safe[0, 0] > 0.5, lambda: (x, res), guarded)


def solution(mesh):
    return jax.shard_map(
        on_device,
        mesh=mesh,
        in_specs=(
            P(None, "azimuth", "span", None),
            P("azimuth", "span", None),
            P("azimuth", "span", None),
            P(None, "azimuth", "span", None),
            P("azimuth", "span", None),
            P("azimuth", "span"),
        ),
        out_specs=(P(None, "azimuth", "span", None), P(None, "azimuth", "span", None)),
        check_vma=False,
    )
```

```python
import jax
import jax.numpy as jnp
from jax import lax
from jax.experimental import pallas as pl
from jax.experimental.pallas import tpu as pltpu
from jax.sharding import PartitionSpec as P


ITERS = 3
penalty_weight = 4.0
SHIFT = 5.0
SAFE = 0.01
F32 = jnp.float32
VMEM = pl.BlockSpec(memory_space=pltpu.VMEM)
SMEM = pl.BlockSpec(memory_space=pltpu.SMEM)


def padded_2(x, sides, width):
    for axis, dim in sides:
        peers, length = (lax.axis_size(axis), x.shape[dim])
        up = [(i, (i + 1) % peers) for i in range(peers)]
        down = [(j, i) for i, j in up]
        last = lax.slice_in_dim(x, length - width, length, axis=dim)
        leading = lax.slice_in_dim(x, 0, width, axis=dim)
        before = lax.ppermute(last, axis, up)
        after = lax.ppermute(leading, axis, down)
        x = jnp.concatenate([before, x, after], axis=dim)
    return x


def ahead(field, axis):
    count = field.shape[axis]
    rest = lax.slice_in_dim(field, 1, count, axis=axis)
    return jnp.concatenate([rest, jnp.zeros_like(lax.slice_in_dim(field, 0, 1, axis=axis))], axis)


def behind(field, axis):
    count = field.shape[axis]
    rest = lax.slice_in_dim(field, 0, count - 1, axis=axis)
    return jnp.concatenate([jnp.zeros_like(lax.slice_in_dim(field, 0, 1, axis=axis)), rest], axis)


def coupling(field, shear, spring):
    return (
        jnp.stack(
            [
                field[0] + shear[0] * field[1] + shear[1] * field[2],
                shear[0] * field[0] + field[1] + shear[2] * field[2],
                shear[1] * field[0] + shear[2] * field[1] + field[2],
            ]
        )
        * spring
    )


def stepwise(sensitivity, stiffness, spring, shear, live, inter):
    _, rows_span, _ = stiffness.shape
    padded = padded_2(jnp.stack([stiffness, live]), (("azimuth", 1), ("span", 2)), 1)
    kpad = padded[0]
    lpad = padded[1]
    w_ap = live * lpad[2:, 1:-1] * (stiffness + kpad[2:, 1:-1]) * 0.5
    w_am = live * lpad[:-2, 1:-1] * (stiffness + kpad[:-2, 1:-1]) * 0.5
    w_sp = live * lpad[1:-1, 2:] * (stiffness + kpad[1:-1, 2:]) * 0.5
    w_sm = live * lpad[1:-1, :-2] * (stiffness + kpad[1:-1, :-2]) * 0.5
    span_rank = lax.axis_index("span")
    span_count = lax.axis_size("span")
    row = lax.broadcasted_iota(jnp.int32, stiffness.shape, 1)
    top_edge = jnp.logical_and(span_rank == span_count - 1, row == rows_span - 1)
    low_edge = jnp.logical_and(span_rank == 0, row == 0)
    w_sp = jnp.where(top_edge, 0.0, w_sp)
    w_sm = jnp.where(low_edge, 0.0, w_sm)
    w_zp = live * ahead(live, 2) * (stiffness + ahead(stiffness, 2)) * 0.5
    w_zm = live * behind(live, 2) * (stiffness + behind(stiffness, 2)) * 0.5
    residual = live * sensitivity
    solution_field = jnp.zeros_like(residual)

    def squares(vector):
        return lax.psum(jnp.sum(vector * vector), ("azimuth", "span"))

    def iteration(step, carry):
        solution_field, residual, direction, norm_now = carry
        extended = padded_2(direction, (("azimuth", 1), ("span", 2)), 1)
        next_az = extended[:, 2:, 1:-1]
        prev_az = extended[:, :-2, 1:-1]
        next_span = extended[:, 1:-1, 2:]
        prev_span = extended[:, 1:-1, :-2]
        lap = w_ap * (direction - next_az) + w_am * (direction - prev_az)
        lap = lap + w_sp * (direction - next_span) + w_sm * (direction - prev_span)
        lap = (
            lap
            + w_zp * (direction - ahead(direction, 3))
            + w_zm * (direction - behind(direction, 3))
        )
        coupled = coupling(direction, shear, spring)
        image = live * (lap + coupled + penalty_weight * inter * direction)
        alpha = norm_now / lax.psum(jnp.sum(direction * image), ("azimuth", "span"))
        solution_field = solution_field + alpha * direction
        residual = residual - alpha * image
        norm_next = squares(residual)
        direction = residual + norm_next / norm_now * direction
        return solution_field, residual, direction, norm_next

    carry = (solution_field, residual, residual, squares(residual))
    carry = lax.fori_loop(0, ITERS, iteration, carry)
    return carry[0], carry[1]


FIELDS = 8
TILE = 8


def call(kernel, shapes, n_in, smem=(), scratch=()):
    return pl.pallas_call(
        kernel,
        out_shape=[jax.ShapeDtypeStruct(s, F32) for s in shapes],
        in_specs=[SMEM if i in smem else VMEM for i in range(n_in)],
        out_specs=[VMEM] * len(shapes),
        scratch_shapes=[pltpu.VMEM(s, F32) for s in scratch],
        compiler_params=pltpu.CompilerParams(vmem_limit_bytes=32 << 20),
    )


def reach(f):
    return 2 if f < 4 else 1


def place(f, d):
    return 2 * f + d - 1 if f < 4 else 4 + f


STRIP = 12
CORNER = 6
RELAY = CORNER + 5


def even(axis):
    return lax.axis_index(axis) % 2 == 0


def sublane(slots):
    return lax.broadcasted_iota(jnp.int32, (TILE, slots), 0)


def turn(x, shift, axis):
    shift = shift % x.shape[axis]
    return pltpu.roll(x, shift, axis) if shift else x


def packed_rows(tiles, sign):
    s = sublane(tiles[0].shape[1])
    s = s if sign > 0 else TILE - 1 - s
    out = [jnp.where(s < 3, tiles[f], turn(tiles[f + 1], sign * 3, 0)) for f in (0, 2)]
    last = tiles[4]
    for j in range(1, 4):
        last = jnp.where(s < 2 * j, last, turn(tiles[4 + j], sign * 2 * j, 0))
    return out + [last]


def unpacked(ref, f, a, sign):
    tile = ref[3 * a + (f // 2 if f < 4 else 2)]
    return turn(tile, -sign * (3 * (f % 2) if f < 4 else 2 * (f - 4)), 0)


def pack_kernel(blocks_ref, s_ref, k_ref, spring_ref, shear_ref, inter_ref, own_ref, me_ref, mo_ref, se_ref, so_ref):
    n_az, n_sp, slots = k_ref.shape
    blocks = inter_ref.shape[1]
    width = slots // blocks
    zpos = lax.broadcasted_iota(jnp.int32, (n_sp, slots), 1)
    live = zpos < jnp.broadcast_to(blocks_ref[...] * width, (n_sp, slots))
    same = lax.broadcasted_iota(jnp.int32, (n_sp, n_sp), 0) == lax.broadcasted_iota(jnp.int32, (n_sp, n_sp), 1)
    for a in range(n_az):
        spring = spring_ref[a]
        flags = inter_ref[a].astype(F32)
        columns = []
        for b in range(blocks):
            row = jnp.broadcast_to(flags[b : b + 1, :], (n_sp, n_sp))
            column = jnp.sum(jnp.where(same, row, 0.0), axis=1, keepdims=True)
            columns.append(jnp.broadcast_to(column, (n_sp, width)))
        inter = jnp.concatenate(columns, axis=1)
        fields = [s_ref[c, a] for c in range(3)] + [k_ref[a], spring + penalty_weight * inter]
        fields += [shear_ref[i, a] * spring for i in range(3)]
        fields = [jnp.where(live, v, 0.0) for v in fields]
        for f, v in enumerate(fields):
            own_ref[f, a] = v
        first = packed_rows([v[:TILE] for v in fields], 1)
        last = packed_rows([v[n_sp - TILE :] for v in fields], -1)
        up = even("span")
        for n in range(3):
            se_ref[3 * a + n] = jnp.where(up, last[n], first[n])
            so_ref[3 * a + n] = jnp.where(up, first[n], last[n])
    flip = even("azimuth")
    for f in range(FIELDS):
        for d in range(1, reach(f) + 1):
            me_ref[place(f, d)] = own_ref[f, jnp.where(flip, n_az - d, d - 1)]
            mo_ref[place(f, d)] = own_ref[f, jnp.where(flip, d - 1, n_az - d)]


def face(k, near):
    return jnp.where(jnp.minimum(k, near) > 0.0, (k + near) * 0.5, 0.0)


def layer_weights(k, lane):
    slots = k.shape[1]
    return face(k, turn(k, -1, 0)), face(k, jnp.where(lane == slots - 1, 0.0, turn(k, -1, 1)))


def local_diagonal(k, ws, wz, fixed):
    return (ws + turn(ws, 1, 0)) + (wz + turn(wz, 1, 1)) + (fixed - jnp.where(k > 0.0, SHIFT, 0.0))


def image_of(get, off, wl, wh, ws, wz, diag, a):
    u = [get(c, a) for c in range(3)]
    mixed = [off[0] * u[1] + off[1] * u[2], off[0] * u[0] + off[2] * u[2], off[1] * u[0] + off[2] * u[1]]
    out = []
    for c in range(3):
        acc = wh * get(c, a + 1) + wl * get(c, a - 1)
        acc = acc + (ws * turn(u[c], -1, 0) + turn(ws * u[c], 1, 0))
        acc = acc + (wz * turn(u[c], -1, 1) + turn(wz * u[c], 1, 1))
        out.append(diag * u[c] + mixed[c] - acc)
    return out


def side_kernel(own, se_ref, so_ref, near_ref, re_ref, ro_ref, u1_ref, wa_ref, ws_ref, wz_ref, diag_ref):
    n_az, n_sp, slots = own.shape[1:]
    s = lax.broadcasted_iota(jnp.int32, (TILE, slots), 0)
    lane = lax.broadcasted_iota(jnp.int32, (n_sp + TILE, slots), 1)
    up, flip = even("span"), even("azimuth")
    for a in range(n_az):
        after = {3 * a + n: jnp.where(up, se_ref[3 * a + n], so_ref[3 * a + n]) for n in range(3)}
        before = {3 * a + n: jnp.where(up, so_ref[3 * a + n], se_ref[3 * a + n]) for n in range(3)}
        for f in range(FIELDS):
            near_ref[f * n_az + a] = jnp.where(
                s < TILE // 2, unpacked(after, f, a, 1), unpacked(before, f, a, -1)
            )

    def field(f, a):
        return jnp.concatenate([own[f, a], near_ref[f * n_az + a]], axis=0)

    for a in range(n_az):
        k = field(3, a)
        ws, wz = layer_weights(k, lane)
        ws_ref[a], wz_ref[a] = ws, wz
        diag = local_diagonal(k, ws, wz, field(4, a))
        if a + 1 < n_az:
            wa_ref[a] = face(k, field(3, a + 1))
            diag = diag + wa_ref[a]
        diag_ref[a] = diag + wa_ref[a - 1] if a > 0 else diag
    for a in range(1, n_az - 1):
        off = [field(5 + i, a) for i in range(3)]
        image = image_of(field, off, wa_ref[a - 1], wa_ref[a], ws_ref[a], wz_ref[a], diag_ref[a], a)
        for c, v in enumerate(image):
            u1_ref[c, a - 1] = v

    def corner(one, step):
        out = []
        for c in range(3):
            v = u1_ref[c, one + step - 1]
            out += [v[:TILE], v[TILE:n_sp]]
        for f in range(4):
            near, far = near_ref[f * n_az + one], near_ref[f * n_az + one + step]
            out.append(jnp.where(s == 2, turn(far, 2, 0), jnp.where(s == TILE - 3, turn(far, -2, 0), near)))
        packed = near_ref[4 * n_az + one]
        for j in range(1, 4):
            v = near_ref[(4 + j) * n_az + one]
            packed = jnp.where(s == j, turn(v, j, 0), jnp.where(s == TILE - 1 - j, turn(v, -j, 0), packed))
        return out + [packed]

    for n, (low, high) in enumerate(zip(corner(0, 1), corner(n_az - 1, -1))):
        re_ref[n] = jnp.where(flip, high, low)
        ro_ref[n] = jnp.where(flip, low, high)


PAIRS = ((0, 0), (0, 1), (0, 2), (0, 3), (1, 1), (1, 2), (1, 3), (2, 2), (2, 3), (3, 3))


def folded(x):
    n, m = x.shape
    x = x.reshape(n // 8, 8, m).sum(0) if n > 8 else x
    out = x[:, 0:128]
    for b in range(1, m // 128):
        out = out + x[:, b * 128 : (b + 1) * 128]
    return out


def basis_kernel(own, near, me, mo, re, ro, *rest):
    flip = even("azimuth")

    @pl.when(flip)
    def _():
        basis(own, near, (mo, ro), (me, re), *rest)

    @pl.when(jnp.logical_not(flip))
    def _():
        basis(own, near, (me, re), (mo, ro), *rest)


def basis(own, near, low, high, mid, wa, ws, wz, diag, u1_ref, u2_ref, u3_ref, sums_ref, wa_out, ws_out, wz_out, diag_out):
    n_az, n_sp, slots = own.shape[1:]
    s = lax.broadcasted_iota(jnp.int32, (TILE, slots), 0)
    lane = lax.broadcasted_iota(jnp.int32, (n_sp + TILE, slots), 1)
    ends = (-1, n_az)

    def field(f, a):
        if 0 <= a < n_az:
            return jnp.concatenate([own[f, a], near[f * n_az + a]], axis=0)
        (side, relay), d = (high, a - n_az + 1) if a >= n_az else (low, -a)
        if f < 4:
            tile = relay[CORNER + f]
            if d == 2:
                tile = jnp.where(s < TILE // 2, turn(tile, -2, 0), turn(tile, 2, 0))
        else:
            j = f - 4
            tile = relay[CORNER + 4]
            tile = jnp.where(s < TILE // 2, turn(tile, -j, 0), turn(tile, j, 0))
        return jnp.concatenate([side[place(f, d)], tile], axis=0)

    outer = {-2: 0, -1: 1, n_az - 1: 2, n_az: 3}
    for a, n in outer.items():
        wa_out[n] = face(field(3, a), field(3, a + 1))
    for n, a in enumerate(ends):
        k = field(3, a)
        ws_out[n], wz_out[n] = layer_weights(k, lane)
        total = local_diagonal(k, ws_out[n], wz_out[n], field(4, a))
        diag_out[n] = total + wa_out[outer[a - 1]] + wa_out[outer[a]]
    diag_out[2] = diag[0] + wa_out[outer[-1]]
    diag_out[3] = diag[n_az - 1] + wa_out[outer[n_az - 1]]

    def between(a):
        return wa_out[outer[a]] if a in outer else wa[a]

    def image(get, a):
        n = ends.index(a) if a in ends else None
        rows, slot = (ws_out[n], wz_out[n]) if a in ends else (ws[a], wz[a])
        middle = diag_out[n] if a in ends else diag_out[2] if a == 0 else diag_out[3] if a == n_az - 1 else diag[a]
        off = [field(5 + i, a) for i in range(3)]
        return image_of(get, off, between(a - 1), between(a), rows, slot, middle, a)

    def first(c, a):
        if 0 < a < n_az - 1:
            return mid[c, a - 1]
        if -1 <= a <= n_az:
            return u1_ref[c, a + 1]
        relay = high[1] if a > 0 else low[1]
        return jnp.concatenate([relay[2 * c], relay[2 * c + 1], jnp.zeros((TILE, slots), F32)], axis=0)

    for a in (-1, 0, n_az - 1, n_az):
        for c, v in enumerate(image(field, a)):
            u1_ref[c, a + 1] = v
    for a in range(-1, n_az + 1):
        for c, v in enumerate(image(first, a)):
            u2_ref[c, a + 1] = v
    acc = [jnp.zeros((8, 128), F32) for _ in PAIRS]
    for a in range(n_az):
        for c, v in enumerate(image(lambda c, b: u2_ref[c, b + 1], a)):
            v = v[:n_sp]
            u3_ref[c, a] = v
            u = [own[c, a], first(c, a)[:n_sp], u2_ref[c, a + 1][:n_sp], v]
            for n, (i, j) in enumerate(PAIRS):
                acc[n] = acc[n] + folded(u[i] * u[j])
    lane = lax.broadcasted_iota(jnp.int32, (8, 128), 1)
    total = jnp.zeros((8, 128), F32)
    for n in range(len(PAIRS)):
        one = jnp.sum(jnp.sum(acc[n], axis=0, keepdims=True), axis=1, keepdims=True)
        total = jnp.where(lane == n, one, total)
    sums_ref[...] = total


def coefficients(rows):
    lane = lax.broadcasted_iota(jnp.int32, (8, 128), 1)
    row = jnp.broadcast_to(jnp.sum(rows, axis=0, keepdims=True), (8, 128))

    def entry(n):
        return jnp.broadcast_to(jnp.sum(jnp.where(lane == n, row, 0.0), axis=1, keepdims=True), (8, 128))

    g = {p: entry(n) for n, p in enumerate(PAIRS)}
    n0 = g[0, 0]
    m10, m20, m30 = g[0, 1] / n0, g[0, 2] / n0, g[0, 3] / n0
    n1 = g[1, 1] - m10 * g[0, 1]
    t21 = g[1, 2] - m10 * g[0, 2]
    t31 = g[1, 3] - m10 * g[0, 3]
    m21, m31 = t21 / n1, t31 / n1
    n2 = g[2, 2] - m20 * g[0, 2] - m21 * t21
    t32 = g[2, 3] - m20 * g[0, 3] - m21 * t31
    m32 = t32 / n2
    n3 = g[3, 3] - m30 * g[0, 3] - m31 * t31 - m32 * t32
    b0, b1, b2 = SHIFT + m10, SHIFT + m21 - m10, SHIFT + m32 - m21
    g1, g2 = n1 / n0, n2 / n1
    a0 = 1.0 / b0
    a1 = 1.0 / (b1 - g1 * a0)
    a2 = 1.0 / (b2 - g2 * a1)
    safe = jnp.logical_and(
        jnp.logical_and(n1 > SAFE * g[1, 1], n2 > SAFE * g[2, 2]),
        jnp.logical_and(n3 > SAFE * g[3, 3], jnp.logical_and(a1 > 0.0, a2 > 0.0)),
    )
    f = {"m10": m10, "m20": m20, "m21": m21, "m30": m30, "m31": m31, "m32": m32}
    f["e1"], f["e2"] = a0 * g1, a1 * g2
    f["x0"], f["x1"], f["x2"] = a0, -(a0 * a1), a0 * a1 * a2
    f["r3"] = -(a0 * a1 * a2)
    return f, safe


def final_kernel(rows_ref, u0_ref, mid_ref, u1_ref, u2_ref, u3_ref, x_ref, r_ref, safe_ref):
    f, safe = coefficients(rows_ref[...])
    safe_ref[...] = jnp.where(safe, 1.0, 0.0)[0:1, 0:1]
    n_az, n_sp, slots = u3_ref.shape[1:]
    f = {key: jnp.concatenate([jnp.concatenate([v] * (n_sp // 8), 0)] * (slots // 128), 1) for key, v in f.items()}
    for c in range(3):
        for a in range(n_az):
            u1 = mid_ref[c, a - 1] if 0 < a < n_az - 1 else u1_ref[c, a + 1]
            u0, u1, u2, u3 = u0_ref[c, a], u1[:n_sp], u2_ref[c, a + 1][:n_sp], u3_ref[c, a]
            q1 = u1 - f["m10"] * u0
            q2 = u2 - f["m21"] * q1 - f["m20"] * u0
            q3 = u3 - f["m32"] * q2 - f["m31"] * q1 - f["m30"] * u0
            p1 = q1 - f["e1"] * u0
            p2 = q2 - f["e2"] * p1
            x_ref[c, a] = f["x0"] * u0 + f["x1"] * p1 + f["x2"] * p2
            r_ref[c, a] = f["r3"] * q3


def swaps(evens, odds, axis, wraps):
    n = lax.axis_size(axis)
    first = [(i, i + 1) for i in range(0, n, 2)]
    second = [(i, (i + 1) % n) for i in range(1, n if wraps else n - 1, 2)]
    out = []
    for v, pairs in ((evens, first), (odds, second)):
        out.append(lax.ppermute(v, axis, pairs + [(j, i) for i, j in pairs]))
    return out


def everywhere(row, axis):
    n = lax.axis_size(axis)
    return lax.all_to_all(jnp.broadcast_to(row, (n, 128)), axis, 0, 0, tiled=True)


def on_device(sensitivity, stiffness, spring, shear, interface, live_blocks):
    rows_az, rows_span, slots = stiffness.shape
    blocks = interface.shape[2]
    width = slots // blocks
    field = (3, rows_az, rows_span, slots)
    strip = (STRIP, rows_span, slots)
    tiles = (3 * rows_az, TILE, slots)
    own, me, mo, se, so = call(pack_kernel, [(FIELDS,) + field[1:], strip, strip, tiles, tiles], 6)(
        live_blocks, sensitivity, stiffness, spring, shear, jnp.transpose(interface, (0, 2, 1))
    )
    se, so = swaps(se, so, "span", False)
    me, mo = swaps(me, mo, "azimuth", True)
    tall = (rows_span + TILE, slots)
    relay = (RELAY, TILE, slots)
    inner = [(rows_az - 1,) + tall] + [(rows_az,) + tall] * 3
    near, re, ro, mid, *weights = call(
        side_kernel, [(FIELDS * rows_az, TILE, slots), relay, relay, (3, rows_az - 2) + tall] + inner, 3
    )(own, se, so)
    re, ro = swaps(re, ro, "azimuth", True)
    u1, u2, u3, sums = call(
        basis_kernel,
        [(3, rows_az + 2) + tall, (3, rows_az + 2) + tall, field, (8, 128)],
        11,
        scratch=((4,) + tall, (2,) + tall, (2,) + tall, (4,) + tall),
    )(own, near, me, mo, re, ro, mid, *weights)
    sums = jnp.sum(everywhere(sums[0:1], "azimuth"), axis=0, keepdims=True)
    rows = everywhere(sums, "span")
    rows, sensitivity, stiffness, spring, shear, interface, live_blocks = lax.optimization_barrier(
        (rows, sensitivity, stiffness, spring, shear, interface, live_blocks)
    )
    x, res, safe = call(final_kernel, [field, field, (1, 1)], 6)(rows, own, mid, u1, u2, u3)

    def guarded():
        zpos = lax.broadcasted_iota(jnp.int32, stiffness.shape, 2)
        live = (zpos < live_blocks[0, 0] * width).astype(F32)
        inter = jnp.broadcast_to(interface[:, :, :, None], (rows_az, rows_span, blocks, width))
        inter = inter.reshape(stiffness.shape).astype(F32)
        return stepwise(sensitivity, stiffness, spring, shear, live, inter)

    return lax.cond(safe[0, 0] > 0.5, lambda: (x, res), guarded)


def solution(mesh):
    return jax.shard_map(
        on_device,
        mesh=mesh,
        in_specs=(
            P(None, "azimuth", "span", None),
            P("azimuth", "span", None),
            P("azimuth", "span", None),
            P(None, "azimuth", "span", None),
            P("azimuth", "span", None),
            P("azimuth", "span"),
        ),
        out_specs=(P(None, "azimuth", "span", None), P(None, "azimuth", "span", None)),
        check_vma=False,
    )
```
